512 devices in a mesh: rep: 16 (over x, y_hi, core), tile: 32 (over y_lo, z).
Axes of the slice: x: 4, y: 8 (y_hi: 2, y_lo: 4; y = y_hi * 4 + y_lo), z: 8, core: 2. Of those that a mesh axis runs over, the one named last changes fastest.
Arguments:
- fields: bfloat16 [16, 192, 8, 8, 256], P('rep', 'tile'), may hold values from -6 to 6
- cotangent: bfloat16 [16, 192, 8, 8, 256], P('rep', 'tile'), may hold values from -6 to 6
- weights: float32 [16, 2304, 256], P('rep', 'tile'), may hold values from -6 to 6
- ema: float32 [16, 2304, 256], P('rep', 'tile'), may hold values from -6 to 6
- tile_links: int32 [192, 4], replicated, may hold values from 0 to 191, as said below
- tile_codes: int32 [192, 4], replicated, may hold values from 0 to 3
- corner_links: int32 [192, 4], replicated, may hold values from -1 to 191, as said below
- corner_codes: int32 [192, 4], replicated, may hold values from 0 to 3
- gossip_bit: int32 [1], replicated, may hold values from 0 to 1
- batch_size: int32 [1], replicated, may hold values from 32 to 512
Outputs:
- activations: bfloat16 [16, 192, 8, 8, 256], P('rep', 'tile')
- field_grad: bfloat16 [16, 192, 8, 8, 256], P('rep', 'tile')
- averaged: float32 [16, 2304, 256], P('rep', 'tile')
- ema_out: float32 [16, 2304, 256], P('rep', 'tile')
The draws below stay inside these ranges and needn't reach their ends.
Inputs may be any that keep to these rules, and one draw needn't show every extreme that they name: tile_links, tile_codes, corner_links and corner_codes describe the tiles of a HEALPix sphere: 12 base faces, each cut into 4 x 4 tiles, numbered face by face (the order of the faces drawn from the seed) and row by row within a face. The relation is symmetric: if tile u lies across edge q of tile t as its edge e, then t lies across edge e of u as its edge q, and cells along a shared edge run in the same order on both tiles; likewise, if corner q of t takes corner cell c of u, then corner c of u takes corner cell q of t. `corner_links`: -1 exactly at the tiles' corners that touch one of the 8 vertices where only three base faces meet.
All inputs are finite; a program needn't handle non-finite values.
Results may differ from the reference program's by a relative error of at most 0.0014.
The reference program's roundings to bfloat16 on the way count: a program that leaves them out, or rounds other values in their place, can miss the bound.
Values may be sent and summed in bfloat16 or wider, within the bound.
No kernel may reach another device: no remote copies, remote signals or barrier semaphores. Data moves between devices by JAX's collectives and lax.ppermute only.
A program may use at most 64 MiB of HBM per device.

```python
import jax
import jax.numpy as jnp
import numpy as np
from jax import lax

C = 256
SUB = 4
TS = 8
TILES = 192
REPS = 16
KROWS = 2304


def face_id(cycle_index, column):
    return cycle_index * 4 + column % 4


def face_cell(face, pos_x, pos_y, span):
    cycle_index = face // 4
    column = face % 4
    last = span - 1
    inside_x = 0 <= pos_x <= last
    inside_y = 0 <= pos_y <= last
    if inside_x and inside_y:
        return (face, pos_x, pos_y)
    if not inside_x and (not inside_y):
        if pos_x > last and pos_y > last:
            if cycle_index == 0:
                return (face_id(0, column + 2), last, last)
            if cycle_index == 2:
                return (face_id(0, column), 0, 0)
            return None
        if pos_x < 0 and pos_y < 0:
            if cycle_index == 0:
                return (face_id(2, column), last, last)
            if cycle_index == 2:
                return (face_id(2, column + 2), 0, 0)
            return None
        if pos_x > last and pos_y < 0:
            if cycle_index == 1:
                return (face_id(1, column + 1), 0, last)
            return None
        if cycle_index == 1:
            return (face_id(1, column - 1), last, 0)
        return None
    if cycle_index == 0:
        if pos_x > last:
            return (face_id(0, column + 1), pos_y, last)
        if pos_y > last:
            return (face_id(0, column - 1), last, pos_x)
        if pos_x < 0:
            return (face_id(1, column), last, pos_y)
        return (face_id(1, column + 1), pos_x, last)
    if cycle_index == 1:
        if pos_x > last:
            return (face_id(0, column), 0, pos_y)
        if pos_y > last:
            return (face_id(0, column - 1), pos_x, 0)
        if pos_x < 0:
            return (face_id(2, column - 1), last, pos_y)
        return (face_id(2, column), pos_x, last)
    if pos_x > last:
        return (face_id(1, column + 1), 0, pos_y)
    if pos_y > last:
        return (face_id(1, column), pos_x, 0)
    if pos_x < 0:
        return (face_id(2, column - 1), pos_y, 0)
    return (face_id(2, column + 1), 0, pos_x)


def sphere_tables():
    tile_side = 4
    span = SUB * tile_side
    per_face = SUB * SUB
    total_tiles = 12 * per_face
    link_table = np.zeros((total_tiles, 4), np.int32)
    code_table = np.zeros((total_tiles, 4), np.int32)
    corner_table = np.zeros((total_tiles, 4), np.int32)
    corner_code_table = np.zeros((total_tiles, 4), np.int32)
    corner_offsets = [(-1, -1), (-1, tile_side), (tile_side, -1), (tile_side, tile_side)]
    for face in range(12):
        for row_block in range(SUB):
            for col_block in range(SUB):
                tile_id = face * per_face + row_block * SUB + col_block
                base_x = row_block * tile_side
                base_y = col_block * tile_side
                for side_id in range(4):
                    found = []
                    for along in range(2):
                        offset = [(-1, along), (tile_side, along), (along, -1), (along, tile_side)][side_id]
                        found.append(face_cell(face, base_x + offset[0], base_y + offset[1], span))
                    other_face, cell_x, cell_y = found[0]
                    link_table[tile_id, side_id] = other_face * per_face + cell_x // tile_side * SUB + cell_y // tile_side
                    local_x = cell_x % tile_side
                    local_y = cell_y % tile_side
                    if found[1][1] == cell_x:
                        code_table[tile_id, side_id] = 0 if local_x == 0 else 1
                    else:
                        code_table[tile_id, side_id] = 2 if local_y == 0 else 3
                for corner_id in range(4):
                    offset = corner_offsets[corner_id]
                    across = face_cell(face, base_x + offset[0], base_y + offset[1], span)
                    if across is None:
                        corner_table[tile_id, corner_id] = -1
                        corner_code_table[tile_id, corner_id] = 0
                    else:
                        other_face, cell_x, cell_y = across
                        corner_table[tile_id, corner_id] = other_face * per_face + cell_x // tile_side * SUB + cell_y // tile_side
                        corner_code_table[tile_id, corner_id] = 2 * int(cell_x % tile_side == tile_side - 1) + int(cell_y % tile_side == tile_side - 1)
    return (link_table, code_table, corner_table, corner_code_table)


def sphere_draw(key):
    link_table, code_table, corner_table, corner_code_table = sphere_tables()
    per_face = SUB * SUB
    column = jax.random.randint(jax.random.fold_in(key, 11), (), 0, 4).astype(jnp.int32)
    first_face = 8 + column
    second_face = 8 + (column + 3) % 4
    face_ids = jnp.arange(12, dtype=jnp.int32)
    scores = jax.random.permutation(jax.random.fold_in(key, 12), 12).astype(jnp.int32)
    scores = jnp.where(face_ids == first_face, 100, jnp.where(face_ids == second_face, 101, scores))
    ranked = jnp.argsort(scores, stable=True).astype(jnp.int32)
    face_at_pos = jnp.concatenate([ranked[10:11], ranked[0:5], ranked[11:12], ranked[5:10]])
    pos_of = jnp.zeros((12,), jnp.int32).at[face_at_pos].set(face_ids)
    tile_ids = jnp.arange(12 * per_face, dtype=jnp.int32)
    faces = tile_ids // per_face
    renamed = pos_of[faces] * per_face + tile_ids % per_face
    empty = jnp.zeros((12 * per_face, 4), jnp.int32)
    links = empty.at[renamed].set(renamed[jnp.asarray(link_table)])
    codes = empty.at[renamed].set(jnp.asarray(code_table))
    corner_base = jnp.asarray(corner_table)
    corner_named = jnp.where(corner_base >= 0, renamed[jnp.maximum(corner_base, 0)], -1)
    corners = empty.at[renamed].set(corner_named)
    corner_codes = empty.at[renamed].set(jnp.asarray(corner_code_table))
    return (links, codes, corners, corner_codes)


def draw_tile_links(key, part):
    return sphere_draw(key)[0]


def draw_tile_codes(key, part):
    return sphere_draw(key)[1]


def draw_corner_links(key, part):
    return sphere_draw(key)[2]


def draw_corner_codes(key, part):
    return sphere_draw(key)[3]


def shard_levels(key, extent, shards, low, high):
    gain = 1.0
    for position, shards_of in shards:
        draws = jax.random.uniform(jax.random.fold_in(jax.random.fold_in(key, 6), position), (shards_of,), jnp.float32, low / len(shards), high / len(shards))
        gain = gain * jnp.repeat(jnp.exp(draws), extent[position] // shards_of).reshape((-1,) + (1,) * (len(extent) - 1 - position))
    return gain


def centred(own_key, dims, width, reach, cuts=(), held_as=jnp.bfloat16):
    entries = jax.random.normal(own_key, dims, jnp.float32) * width
    if len(cuts) > 0:
        entries = shard_levels(own_key, dims, cuts, -0.22, 0.18) * entries
    return jnp.clip(entries, min=-reach, max=reach).astype(held_as)


def setup_inputs(seed: int = 0) -> dict:
    key_of = jax.random.split(jax.random.key(seed), 11)
    fields = centred(key_of[0], (REPS, TILES, TS, TS, C), 1.0, 6.0, ((0, 16), (1, 32)))
    cotangent = centred(key_of[1], (REPS, TILES, TS, TS, C), 1.0, 6.0, ((0, 16), (1, 32)))
    weights = centred(key_of[2], (REPS, KROWS, C), 1.0, 6.0, ((0, 16), (1, 32)), jnp.float32)
    ema = centred(key_of[3], (REPS, KROWS, C), 1.0, 6.0, ((0, 16), (1, 32)), jnp.float32)
    tile_links = draw_tile_links(jax.random.fold_in(key_of[10], 71), 0)
    tile_codes = draw_tile_codes(jax.random.fold_in(key_of[10], 71), 0)
    corner_links = draw_corner_links(jax.random.fold_in(key_of[10], 71), 0)
    corner_codes = draw_corner_codes(jax.random.fold_in(key_of[10], 71), 0)
    gossip_bit = jax.random.randint(key_of[8], (1,), 0, 2).astype(jnp.int32)
    batch_size = jax.random.randint(key_of[9], (1,), 32, 513).astype(jnp.int32)
    return dict(fields=fields, cotangent=cotangent, weights=weights, ema=ema, tile_links=tile_links, tile_codes=tile_codes, corner_links=corner_links, corner_codes=corner_codes, gossip_bit=gossip_bit, batch_size=batch_size)


LEARN = 0.5

def edge_strips(block):
    return jnp.stack([block[:, 0], block[:, -1], block[:, :, 0], block[:, :, -1]], axis=1)

def corner_cells(block):
    return jnp.stack([block[:, 0, 0], block[:, 0, -1], block[:, -1, 0], block[:, -1, -1]], axis=1)

def padded_sides(block):
    return jnp.stack([block[:, 0, 1:-1], block[:, -1, 1:-1], block[:, 1:-1, 0], block[:, 1:-1, -1]], axis=1)

def with_halo(block, strips, corner_vals):
    top_row = jnp.concatenate([corner_vals[:, 0:1], strips[:, 0], corner_vals[:, 1:2]], axis=1)
    bottom_row = jnp.concatenate([corner_vals[:, 2:3], strips[:, 1], corner_vals[:, 3:4]], axis=1)
    middle = jnp.concatenate([strips[:, 2][:, :, None], block, strips[:, 3][:, :, None]], axis=2)
    return jnp.concatenate([top_row[:, None], middle, bottom_row[:, None]], axis=1)

def reference(fields, cotangent, weights, ema, tile_links, tile_codes, corner_links, corner_codes, gossip_bit, batch_size):
    present = (corner_links >= 0)[:, :, None]
    corner_source = jnp.maximum(corner_links, 0)
    weight_scale = (9.0 * C) ** (-0.5)

    def one_replica(packed):
        field_block, cot_block, weight_rows = packed
        kernel = (weight_rows * weight_scale).astype(jnp.bfloat16).reshape(C, 9, C)
        strips = edge_strips(field_block)[tile_links, tile_codes]
        corner_vals = jnp.where(present, corner_cells(field_block)[corner_source, corner_codes], jnp.zeros((), jnp.bfloat16))
        padded = with_halo(field_block, strips, corner_vals)
        hidden = jnp.zeros((TILES * TS * TS, C), jnp.float32)
        for tap_index in range(9):
            row_off, col_off = divmod(tap_index, 3)
            window = padded[:, row_off:row_off + TS, col_off:col_off + TS].reshape(-1, C)
            hidden = hidden + jnp.dot(window, kernel[:, tap_index, :], preferred_element_type=jnp.float32)
        sigmoid_pre = jax.nn.sigmoid(hidden)
        output = (hidden * sigmoid_pre).astype(jnp.bfloat16)
        grad_pre = (cot_block.reshape(-1, C).astype(jnp.float32) * (sigmoid_pre * (1.0 + hidden * (1.0 - sigmoid_pre)))).astype(jnp.bfloat16)
        pieces = []
        grad_pad = jnp.zeros((TILES, TS + 2, TS + 2, C), jnp.float32)
        for tap_index in range(9):
            row_off, col_off = divmod(tap_index, 3)
            window = padded[:, row_off:row_off + TS, col_off:col_off + TS].reshape(-1, C)
            pieces.append(jnp.dot(window.T, grad_pre, preferred_element_type=jnp.float32))
            backward = jnp.dot(grad_pre, kernel[:, tap_index, :].T, preferred_element_type=jnp.float32)
            grad_pad = grad_pad.at[:, row_off:row_off + TS, col_off:col_off + TS].add(backward.reshape(TILES, TS, TS, C))
        kernel_grad = jnp.stack(pieces, axis=1).reshape(9 * C, C)
        side_grad = lax.optimization_barrier(padded_sides(grad_pad).astype(jnp.bfloat16)).astype(jnp.float32)
        corner_grad = jnp.where(present, corner_cells(grad_pad), jnp.zeros((), jnp.float32))
        corner_grad = lax.optimization_barrier(corner_grad.astype(jnp.bfloat16)).astype(jnp.float32)
        returned = jnp.zeros((TILES, 4, TS, C), jnp.float32).at[tile_links, tile_codes].add(side_grad)
        corner_back = jnp.zeros((TILES, 4, C), jnp.float32).at[corner_source, corner_codes].add(corner_grad)
        interior = grad_pad[:, 1:-1, 1:-1]
        interior = interior.at[:, 0].add(returned[:, 0]).at[:, -1].add(returned[:, 1])
        interior = interior.at[:, :, 0].add(returned[:, 2]).at[:, :, -1].add(returned[:, 3])
        interior = interior.at[:, 0, 0].add(corner_back[:, 0]).at[:, 0, -1].add(corner_back[:, 1])
        interior = interior.at[:, -1, 0].add(corner_back[:, 2]).at[:, -1, -1].add(corner_back[:, 3])
        square_sum = jnp.sum(kernel_grad * kernel_grad)
        root_mean = jnp.sqrt(square_sum / (9.0 * C * C) + 1e-06)
        updated = weight_rows - LEARN * kernel_grad / root_mean
        return (output.reshape(TILES, TS, TS, C), interior.astype(jnp.bfloat16), updated)
    outputs, field_grads, updated = lax.map(one_replica, (fields, cotangent, weights))
    partner_ids = jnp.bitwise_xor(jnp.arange(REPS, dtype=jnp.int32), jnp.left_shift(jnp.int32(1), gossip_bit[0]))
    averaged = 0.5 * (updated + updated[partner_ids])
    decay = jnp.power(0.99, batch_size[0].astype(jnp.float32) / 32.0)
    ema_out = decay * ema + (1.0 - decay) * averaged
    return (outputs, field_grads, averaged, ema_out)
```

```python
import jax
import jax.numpy as jnp
from jax import lax
from jax.experimental import pallas as pl
from jax.experimental.pallas import tpu as pltpu
from jax.sharding import PartitionSpec as P

LEARN = 0.5
STRIPS = 5
HALO = STRIPS + 1
F32 = jnp.float32
BF16 = jnp.bfloat16
SMEM = pltpu.SMEM


def rows_iota(shape):
    return lax.broadcasted_iota(jnp.int32, shape, len(shape) - 2)


def pick_row(group, row):
    return jnp.sum(jnp.where(rows_iota(group.shape) == row, group, 0.0), axis=0, keepdims=True)


def count_bits(v):
    v = v - ((v >> 1) & 0x55555555)
    v = (v & 0x33333333) + ((v >> 2) & 0x33333333)
    v = (v + (v >> 4)) & 0x0F0F0F0F
    return (v * 0x01010101) >> 24


def link_of(entry):
    return entry & 255


def code_of(entry):
    return (entry >> 8) & 3


def slot_of(entry):
    return (entry >> 10) & 31


def owner_of(entry):
    return entry >> 16


def build_routes(me, links, codes, route, masks, base, per, width):
    def clear(d, c):
        masks[d] = 0
        return c

    lax.fori_loop(0, width + 1, clear, 0)

    def owner_and_bit(k):
        tile = me * per + (k >> 2)
        link = links[k & 3, tile]
        code = codes[k & 3, tile]
        owner = jnp.where(link < 0, width, (link * 10923) >> 16)
        bit = jnp.where(me < owner, k, (link - owner * per) * 4 + code)
        bit = jnp.where(link < 0, 0, bit)
        return link, code, owner, bit

    def mark(k, c):
        _, _, owner, bit = owner_and_bit(k)
        masks[owner] = masks[owner] | (1 << bit)
        return c

    lax.fori_loop(0, 4 * per, mark, 0)

    def number(k, c):
        link, code, owner, bit = owner_and_bit(k)
        slot = count_bits(masks[owner] & ((1 << bit) - 1))
        route[base + k] = (link & 255) | (code << 8) | (slot << 10) | (owner << 16)
        return c

    lax.fori_loop(0, 4 * per, number, 0)


def pack_kernel(me_ref, tl, tc, cl, cc, field, rows, send, strips, route, masks, taps, low, high):
    per, side = field.shape[0], field.shape[1]
    width = send.shape[0]
    entries = 4 * per
    me = me_ref[0]
    build_routes(me, tl, tc, route, masks, 0, per, width)
    build_routes(me, cl, cc, route, masks, entries, per, width)
    scale = (9.0 * rows.shape[1]) ** (-0.5)
    half = rows.shape[1] // 2
    for n, part in enumerate((low, high)):
        part[...] = rows[:, n * half : (n + 1) * half]
    for tap in range(9):
        picked = [part[pl.ds(tap, 8, stride=9), :] for part in (low, high)]
        taps[tap] = (jnp.concatenate(picked, axis=1) * scale).astype(BF16)
    zero = jnp.zeros(taps.shape[1:], BF16)

    def spread(d, c):
        send[d, pl.ds(0, 9)] = taps[...]
        send[d, 9 + STRIPS] = zero
        return c

    lax.fori_loop(0, width, spread, 0)

    def edges(t, c):
        strips[t, 0] = field[t, 0]
        strips[t, 1] = field[t, side - 1]
        shape = (side, field.shape[3])
        where = rows_iota(shape)
        left = jnp.zeros(shape, F32)
        right = jnp.zeros(shape, F32)
        for i in range(side):
            x = field[t, i].astype(F32)
            left = jnp.where(where == i, jnp.broadcast_to(x[0:1], shape), left)
            right = jnp.where(where == i, jnp.broadcast_to(x[side - 1 : side], shape), right)
        strips[t, 2] = left.astype(BF16)
        strips[t, 3] = right.astype(BF16)
        return c

    lax.fori_loop(0, per, edges, 0)

    def place(k, c):
        entry = route[k]

        @pl.when(owner_of(entry) != me)
        def _():
            send[owner_of(entry), 9 + slot_of(entry)] = strips[k >> 2, k & 3]

        corner = route[entries + k]
        owner = owner_of(corner)

        @pl.when((owner != me) & (owner < width))
        def _():
            q = k & 3
            cell = pick_row(strips[k >> 2, q >> 1].astype(F32), (q & 1) * (side - 1))
            old = send[owner, 9 + STRIPS].astype(F32)
            new = jnp.where(rows_iota(old.shape) == slot_of(corner), cell, old)
            send[owner, 9 + STRIPS] = new.astype(BF16)

        return c

    lax.fori_loop(0, entries, place, 0)


def conv_kernel(
    me_ref, route, field, strips, cot, recv, act, send, inner, own_sides, own_corners,
    pad0, pad1, pad2, taps, dpre, acc0, acc1, acc2,
):
    per, side = field.shape[0], field.shape[1]
    width, chans = recv.shape[0], field.shape[3]
    entries = 4 * per
    pairs = per // 2
    me = me_ref[0]
    where = rows_iota((side, chans))

    def near(owner, link, code, slot):
        mine = owner == me
        here = strips[jnp.where(mine, link - me * per, 0), code]
        there = recv[jnp.where(mine, 0, owner), 9 + jnp.where(mine, 0, slot)]
        return jnp.where(mine, here.astype(F32), there.astype(F32))

    def halo(p, c):
        tops, bottoms, lefts, rights, cells = [], [], [], [], []
        for h in range(2):
            t = 2 * p + h
            sides = []
            for e in range(4):
                entry = route[t * 4 + e]
                sides.append(
                    near(owner_of(entry), link_of(entry), code_of(entry), slot_of(entry))
                )
            corner_rows = []
            for q in range(4):
                entry = route[entries + t * 4 + q]
                owner = owner_of(entry)
                mine = owner == me
                lost = owner >= width
                code = code_of(entry)
                here = strips[jnp.where(mine, link_of(entry) - me * per, 0), code >> 1]
                there = recv[jnp.where(mine | lost, 0, owner), 9 + STRIPS]
                group = jnp.where(mine, here.astype(F32), there.astype(F32))
                row = jnp.where(mine, (code & 1) * (side - 1), slot_of(entry))
                row = jnp.where(lost, -1, row)
                corner_rows.append(pick_row(group, row))
            tops.append(sides[0])
            bottoms.append(sides[1])
            lefts.append(sides[2])
            rights.append(sides[3])
            cells.append(corner_rows)
        for r in range(side + 2):
            shifted = ([], [], [])
            for h in range(2):
                if r == 0:
                    x, before, after = tops[h], cells[h][0], cells[h][1]
                elif r == side + 1:
                    x, before, after = bottoms[h], cells[h][2], cells[h][3]
                else:
                    x = field[2 * p + h, r - 1].astype(F32)
                    before, after = lefts[h][r - 1 : r], rights[h][r - 1 : r]
                shifted[0].append(jnp.where(where == 0, before, pltpu.roll(x, 1, 0)))
                shifted[1].append(x)
                shifted[2].append(jnp.where(where == side - 1, after, pltpu.roll(x, side - 1, 0)))
            for pad, halves in zip((pad0, pad1, pad2), shifted):
                pad[p, r] = jnp.concatenate(halves, axis=0).astype(BF16)
        return c

    lax.fori_loop(0, pairs, halo, 0)
    for tap in range(9):
        taps[tap] = recv[:, tap].astype(F32).reshape(chans, chans).astype(BF16)

    pads = (pad0, pad1, pad2)
    cells = per * side * side

    def window(tap):
        a, b = divmod(tap, 3)
        return pads[b][:, a : a + side].reshape(cells, chans)

    pre = jnp.zeros((cells, chans), F32)
    for tap in range(9):
        pre = pre + jnp.dot(window(tap), taps[tap], preferred_element_type=F32)
    gate = jax.nn.sigmoid(pre)
    out = (pre * gate).reshape(pairs, side, 2, side, chans)
    slope = (gate * (1.0 + pre * (1.0 - gate))).reshape(pairs, side, 2, side, chans)
    for p in range(pairs):
        for h in range(2):
            act[2 * p + h] = out[p, :, h].astype(BF16)
        grads = [
            cot[2 * p + h].astype(F32) * slope[p, :, h] for h in range(2)
        ]
        for i in range(side):
            dpre[p, i] = jnp.concatenate([grads[0][i], grads[1][i]], axis=0).astype(BF16)
    flat = dpre[...].reshape(cells, chans)
    for tap in range(9):
        part = lax.dot_general(
            window(tap), flat, (((0,), (0,)), ((), ())), preferred_element_type=F32
        )
        high = part.astype(BF16)
        low = part - high.astype(F32)
        send[:, HALO + 2 * tap] = part.reshape(width, 8, chans).astype(BF16)
        send[:, HALO + 2 * tap + 1] = low.reshape(width, 8, chans).astype(BF16)
    accs = (acc0, acc1, acc2)
    for acc in accs:
        acc[...] = jnp.zeros_like(acc)
    for tap in range(9):
        a, b = divmod(tap, 3)
        back = lax.dot_general(
            flat, taps[tap], (((1,), (1,)), ((), ())), preferred_element_type=F32
        )
        accs[b][:, a : a + side] += back.reshape(pairs, side, 2 * side, chans)

    def clear(d, c):
        send[d, STRIPS] = jnp.zeros((8, chans), BF16)
        return c

    lax.fori_loop(0, width, clear, 0)

    def borders(p, c):
        for h in range(2):
            t = 2 * p + h
            span = slice(h * side, (h + 1) * side)
            left = jnp.zeros((side, chans), F32)
            right = jnp.zeros((side, chans), F32)
            corner = jnp.zeros((side, chans), F32)
            for r in range(side + 2):
                q0, q1, q2 = (acc[p, r, span] for acc in accs)
                up = jnp.where(where == side - 1, 0.0, pltpu.roll(q0, side - 1, 0))
                down = jnp.where(where == 0, 0.0, pltpu.roll(q2, 1, 0))
                mid = up + q1 + down
                first = jnp.broadcast_to(q0[0:1], (side, chans))
                last = jnp.broadcast_to(q2[side - 1 : side], (side, chans))
                if r == 0 or r == side + 1:
                    e = 0 if r == 0 else 1
                    own_sides[t, e] = mid.astype(BF16)
                    corner = jnp.where(where == 2 * e, first, corner)
                    corner = jnp.where(where == 2 * e + 1, last, corner)
                else:
                    inner[t, r - 1] = mid
                    left = jnp.where(where == r - 1, first, left)
                    right = jnp.where(where == r - 1, last, right)
            own_sides[t, 2] = left.astype(BF16)
            own_sides[t, 3] = right.astype(BF16)
            own_corners[t] = corner.astype(BF16)
        return c

    lax.fori_loop(0, pairs, borders, 0)

    def place(k, c):
        entry = route[k]

        @pl.when(owner_of(entry) != me)
        def _():
            send[owner_of(entry), slot_of(entry)] = own_sides[k >> 2, k & 3]

        corner = route[entries + k]
        owner = owner_of(corner)

        @pl.when((owner != me) & (owner < width))
        def _():
            cell = pick_row(own_corners[k >> 2].astype(F32), k & 3)
            old = send[owner, STRIPS].astype(F32)
            new = jnp.where(rows_iota(old.shape) == slot_of(corner), cell, old)
            send[owner, STRIPS] = new.astype(BF16)

        return c

    lax.fori_loop(0, entries, place, 0)


def sum_kernel(recv, rows, squares, total):
    step = pl.program_id(0)
    here = recv.shape[1] // 2

    @pl.when(step == 0)
    def _():
        total[...] = jnp.zeros_like(total)

    for j in range(here):
        g = jnp.sum(recv[:, 2 * j].astype(F32) + recv[:, 2 * j + 1].astype(F32), axis=0)
        rows[step * here + j] = g
        total[...] += g * g
    squares[...] = jnp.full(squares.shape, jnp.sum(total[...]), F32)


def grad_kernel(me_ref, route, inner, own_sides, own_corners, recv, out):
    per, side, chans = inner.shape[0], inner.shape[1], inner.shape[3]
    width = recv.shape[0]
    entries = 4 * per
    me = me_ref[0]
    where = rows_iota((side, chans))

    def tile(t, c):
        sides = []
        for e in range(4):
            entry = route[t * 4 + e]
            owner = owner_of(entry)
            mine = owner == me
            here = own_sides[jnp.where(mine, link_of(entry) - me * per, 0), code_of(entry)]
            there = recv[jnp.where(mine, 0, owner), jnp.where(mine, 0, slot_of(entry))]
            sides.append(jnp.where(mine, here.astype(F32), there.astype(F32)))
        cells = []
        for q in range(4):
            entry = route[entries + t * 4 + q]
            owner = owner_of(entry)
            mine = owner == me
            lost = owner >= width
            here = own_corners[jnp.where(mine, link_of(entry) - me * per, 0)]
            there = recv[jnp.where(mine | lost, 0, owner), STRIPS]
            group = jnp.where(mine, here.astype(F32), there.astype(F32))
            row = jnp.where(lost, -1, jnp.where(mine, code_of(entry), slot_of(entry)))
            cells.append(pick_row(group, row))
        for i in range(side):
            x = inner[t, i]
            if i == 0:
                x = x + sides[0]
            if i == side - 1:
                x = x + sides[1]
            first, last = sides[2][i : i + 1], sides[3][i : i + 1]
            x = x + jnp.where(where == 0, first, jnp.where(where == side - 1, last, 0.0))
            if i == 0 or i == side - 1:
                q = 0 if i == 0 else 2
                x = x + jnp.where(
                    where == 0, cells[q], jnp.where(where == side - 1, cells[q + 1], 0.0)
                )
            out[t, i] = x.astype(BF16)
        return c

    lax.fori_loop(0, per, tile, 0)


def body(
    fields, cotangent, weights, ema, tile_links, tile_codes, corner_links, corner_codes,
    gossip_bit, batch_size,
):
    field, cot, w = fields[0], cotangent[0], weights[0]
    per, side, chans = field.shape[0], field.shape[1], field.shape[3]
    width = lax.axis_size("tile")
    reps = lax.axis_size("rep")
    entries = 4 * per
    me = lax.axis_index("tile").astype(jnp.int32).reshape(1)
    smem = pl.BlockSpec(memory_space=SMEM)
    vmem = pl.BlockSpec(memory_space=pltpu.VMEM)
    sds = jax.ShapeDtypeStruct

    def swap(value, bit):
        pairs = [(i, i ^ (1 << bit)) for i in range(reps)]
        return lax.ppermute(value, "rep", pairs)

    def partner(value):
        return jnp.where(gossip_bit[0] == 0, swap(value, 0), swap(value, 1))

    w_partner = partner(w)

    send, strips, route = pl.pallas_call(
        pack_kernel,
        name="pack",
        out_shape=(
            sds((width, 9 + HALO, 8, chans), BF16),
            sds((per, 4, side, chans), BF16),
            sds((2 * entries,), jnp.int32),
        ),
        in_specs=[smem] * 5 + [vmem] * 2,
        out_specs=(vmem, vmem, smem),
        scratch_shapes=[
            SMEM((width + 1,), jnp.int32),
            pltpu.VMEM((9, 8, chans), BF16),
            pltpu.VMEM((72, chans // 2), F32),
            pltpu.VMEM((72, chans // 2), F32),
        ],
    )(me, tile_links.T, tile_codes.T, corner_links.T, corner_codes.T, field, w)

    recv = lax.all_to_all(send, "tile", 0, 0, tiled=True)

    pad = pltpu.VMEM((per // 2, side + 2, 2 * side, chans), BF16)
    acc = pltpu.VMEM((per // 2, side + 2, 2 * side, chans), F32)
    act, send, inner, own_sides, own_corners = pl.pallas_call(
        conv_kernel,
        name="conv",
        out_shape=(
            sds((per, side, side, chans), BF16),
            sds((width, HALO + 18, 8, chans), BF16),
            sds((per, side, side, chans), F32),
            sds((per, 4, side, chans), BF16),
            sds((per, 8, chans), BF16),
        ),
        in_specs=[smem] * 2 + [vmem] * 4,
        out_specs=(vmem,) * 5,
        scratch_shapes=[
            pad, pad, pad,
            pltpu.VMEM((9, chans, chans), BF16),
            pltpu.VMEM((per // 2, side, 2 * side, chans), BF16),
            acc, acc, acc,
        ],
    )(me, route, field, strips, cot, recv)

    recv = lax.all_to_all(send, "tile", 0, 0, tiled=True)

    grouped, squares = pl.pallas_call(
        sum_kernel,
        name="sum",
        grid=(3,),
        out_shape=(sds((9, 8, chans), F32), sds((width, 1, 128), F32)),
        in_specs=[pl.BlockSpec((width, 6, 8, chans), lambda i: (0, i + 1, 0, 0))],
        out_specs=(
            pl.BlockSpec((9, 8, chans), lambda i: (0, 0, 0)),
            pl.BlockSpec((width, 1, 128), lambda i: (0, 0, 0)),
        ),
        scratch_shapes=[pltpu.VMEM((8, chans), F32)],
    )(recv)
    g_partner = partner(grouped)
    total = jnp.sum(lax.all_to_all(squares, "tile", 0, 0, tiled=True)[:, 0, :], axis=0)
    total_partner = partner(total)

    field_grad = pl.pallas_call(
        grad_kernel,
        name="grad",
        grid=(1,),
        out_shape=sds((per, side, side, chans), BF16),
        in_specs=[smem] * 2
        + [vmem] * 3
        + [pl.BlockSpec((width, HALO, 8, chans), lambda i: (0, 0, 0, 0))],
        out_specs=vmem,
    )(me, route, inner, own_sides, own_corners, recv)

    def ordered(value):
        return value.transpose(1, 0, 2).reshape(72, chans)

    def rms(value):
        return jnp.sqrt(value[0] / (9.0 * chans * chans) + 1e-06)

    updated = w - LEARN * ordered(grouped) / rms(total)
    updated_partner = w_partner - LEARN * ordered(g_partner) / rms(total_partner)
    averaged = 0.5 * (updated + updated_partner)
    decay = jnp.power(0.99, batch_size[0].astype(F32) / 32.0)
    ema_out = decay * ema[0] + (1.0 - decay) * averaged
    return act[None], field_grad[None], averaged[None], ema_out[None]


def solution(mesh):
    tiles = P("rep", "tile", None, None, None)
    rows = P("rep", "tile", None)
    return jax.shard_map(
        body,
        mesh=mesh,
        in_specs=(tiles, tiles, rows, rows) + (P(),) * 6,
        out_specs=(tiles, tiles, rows, rows),
        check_vma=False,
    )
```

```python
import jax
import jax.numpy as jnp
from jax import lax
from jax.experimental import pallas as pl
from jax.experimental.pallas import tpu as pltpu
from jax.sharding import PartitionSpec as P


LEARN = 0.5
STRIPS = 5
HALO = STRIPS + 1
F32 = jnp.float32
BF16 = jnp.bfloat16
SMEM = pltpu.SMEM


def rows_iota(shape):
    return lax.broadcasted_iota(jnp.int32, shape, len(shape) - 2)


def pick_row(group, row):
    return jnp.sum(jnp.where(rows_iota(group.shape) == row, group, 0.0), axis=0, keepdims=True)


def count_bits(v):
    v = v - ((v >> 1) & 0x55555555)
    v = (v & 0x33333333) + ((v >> 2) & 0x33333333)
    v = (v + (v >> 4)) & 0x0F0F0F0F
    return (v * 0x01010101) >> 24


def link_of(entry):
    return entry & 255


def code_of(entry):
    return (entry >> 8) & 3


def slot_of(entry):
    return (entry >> 10) & 31


def owner_of(entry):
    return entry >> 16


def build_routes(me, links, codes, route, masks, base, per, width):
    def clear(d, c):
        masks[d] = 0
        return c

    lax.fori_loop(0, width + 1, clear, 0)

    def owner_and_bit(k):
        tile = me * per + (k >> 2)
        link = links[k & 3, tile]
        code = codes[k & 3, tile]
        owner = jnp.where(link < 0, width, (link * 10923) >> 16)
        bit = jnp.where(me < owner, k, (link - owner * per) * 4 + code)
        bit = jnp.where(link < 0, 0, bit)
        return link, code, owner, bit

    def mark(k, c):
        _, _, owner, bit = owner_and_bit(k)
        masks[owner] = masks[owner] | (1 << bit)
        return c

    lax.fori_loop(0, 4 * per, mark, 0)

    def number(k, c):
        link, code, owner, bit = owner_and_bit(k)
        slot = count_bits(masks[owner] & ((1 << bit) - 1))
        route[base + k] = (link & 255) | (code << 8) | (slot << 10) | (owner << 16)
        return c

    lax.fori_loop(0, 4 * per, number, 0)


def taps_kernel(rows, send, low, high):
    scale = (9.0 * rows.shape[1]) ** (-0.5)
    half = rows.shape[1] // 2
    for n, part in enumerate((low, high)):
        part[...] = rows[:, n * half : (n + 1) * half]
    for tap in range(9):
        picked = [part[pl.ds(tap, 8, stride=9), :] for part in (low, high)]
        value = (jnp.concatenate(picked, axis=1) * scale).astype(BF16)
        for n in range(send.shape[0]):
            send[n, tap] = value


def edge_kernel(me_ref, tl, tc, cl, cc, field, send, strips, route, masks):
    per, side = field.shape[0], field.shape[1]
    width = send.shape[0]
    entries = 4 * per
    me = me_ref[0]
    build_routes(me, tl, tc, route, masks, 0, per, width)
    build_routes(me, cl, cc, route, masks, entries, per, width)
    zero = jnp.zeros(send.shape[2:], BF16)

    def clear(d, c):
        send[d, STRIPS] = zero
        return c

    lax.fori_loop(0, width, clear, 0)

    def edges(t, c):
        strips[t, 0] = field[t, 0]
        strips[t, 1] = field[t, side - 1]
        shape = (side, field.shape[3])
        where = rows_iota(shape)
        left = jnp.zeros(shape, F32)
        right = jnp.zeros(shape, F32)
        for i in range(side):
            x = field[t, i].astype(F32)
            left = jnp.where(where == i, jnp.broadcast_to(x[0:1], shape), left)
            right = jnp.where(where == i, jnp.broadcast_to(x[side - 1 : side], shape), right)
        strips[t, 2] = left.astype(BF16)
        strips[t, 3] = right.astype(BF16)
        return c

    lax.fori_loop(0, per, edges, 0)

    def place(k, c):
        entry = route[k]

        @pl.when(owner_of(entry) != me)
        def _():
            send[owner_of(entry), slot_of(entry)] = strips[k >> 2, k & 3]

        corner = route[entries + k]
        owner = owner_of(corner)

        @pl.when((owner != me) & (owner < width))
        def _():
            q = k & 3
            cell = pick_row(strips[k >> 2, q >> 1].astype(F32), (q & 1) * (side - 1))
            old = send[owner, STRIPS].astype(F32)
            new = jnp.where(rows_iota(old.shape) == slot_of(corner), cell, old)
            send[owner, STRIPS] = new.astype(BF16)

        return c

    lax.fori_loop(0, entries, place, 0)


def seat(role, number):
    y = 2 * (number >> 2) + (role >> 1)
    z = 4 * ((number >> 1) & 1) + 2 * (number & 1) + (role & 1)
    return 8 * y + z


PEERS = [[seat(m, n) for n in range(8)] for m in range(4)]
COLUMNS = 30
GRADS = 42
MESSAGE = 138


def place_of(device):
    y, z = divmod(device, 8)
    return 2 * (y & 1) + (z & 1), 4 * (y >> 1) + 2 * (z >> 2) + ((z >> 1) & 1)


def kernel_of(rows, tap):
    parts = []
    for device in range(32):
        role, number = place_of(device)
        parts.append(rows[role, number, tap].astype(F32))
    return jnp.concatenate(parts, axis=0).astype(BF16)


def role_of(me):
    return 2 * ((me >> 3) & 1) + (me & 1)


def forward_kernel(
    me_ref, route, field, strips, cot, recv, rows0, rows1, rows2, rows3,
    act, dpre, taps, message0, message1, message2, message3,
    pad0, pad1, pad2, cols, rows, sems,
):
    per, side = field.shape[0], field.shape[1]
    width, chans = recv.shape[0], field.shape[3]
    entries = 4 * per
    pairs = per // 2
    me = me_ref[0]
    role = role_of(me)
    messages = (message0, message1, message2, message3)
    copies = [
        pltpu.make_async_copy(source, rows.at[role ^ k], sems.at[k])
        for k, source in enumerate((rows0, rows1, rows2, rows3))
    ]
    for copy in copies:
        copy.start()
    where = rows_iota((side, chans))

    def near(owner, link, code, slot):
        mine = owner == me
        here = strips[jnp.where(mine, link - me * per, 0), code]
        there = recv[jnp.where(mine, 0, owner), jnp.where(mine, 0, slot)]
        return jnp.where(mine, here.astype(F32), there.astype(F32))

    def halo(p, c):
        sides, cells = [], []
        for h in range(2):
            t = 2 * p + h
            found = []
            for e in range(4):
                entry = route[t * 4 + e]
                found.append(
                    near(owner_of(entry), link_of(entry), code_of(entry), slot_of(entry))
                )
            corner_rows = []
            for q in range(4):
                entry = route[entries + t * 4 + q]
                owner = owner_of(entry)
                mine = owner == me
                lost = owner >= width
                code = code_of(entry)
                here = strips[jnp.where(mine, link_of(entry) - me * per, 0), code >> 1]
                there = recv[jnp.where(mine | lost, 0, owner), STRIPS]
                group = jnp.where(mine, here.astype(F32), there.astype(F32))
                row = jnp.where(mine, (code & 1) * (side - 1), slot_of(entry))
                row = jnp.where(lost, -1, row)
                corner_rows.append(pick_row(group, row))
            sides.append(found)
            cells.append(corner_rows)
        for h in range(2):
            for n in range(2):
                column, above, below = sides[h][2 + n], cells[h][n], cells[h][2 + n]
                upper = jnp.where(where == 0, above, pltpu.roll(column, 1, 0))
                lower = jnp.where(where == 0, column[side - 1 : side], 0.0)
                lower = jnp.where(where == 1, below, lower)
                cols[n, p, h] = jnp.concatenate([upper, lower], axis=0).astype(BF16)
        for r in range(side + 2):
            shifted = ([], [], [])
            for h in range(2):
                if r == 0:
                    x, before, after = sides[h][0], cells[h][0], cells[h][1]
                elif r == side + 1:
                    x, before, after = sides[h][1], cells[h][2], cells[h][3]
                else:
                    x = field[2 * p + h, r - 1].astype(F32)
                    before, after = sides[h][2][r - 1 : r], sides[h][3][r - 1 : r]
                shifted[0].append(jnp.where(where == 0, before, pltpu.roll(x, 1, 0)))
                shifted[1].append(x)
                shifted[2].append(jnp.where(where == side - 1, after, pltpu.roll(x, side - 1, 0)))
            for pad, halves in zip((pad0, pad1, pad2), shifted):
                pad[p, r] = jnp.concatenate(halves, axis=0).astype(BF16)
        return c

    lax.fori_loop(0, pairs, halo, 0)

    for copy in copies:
        copy.wait()
    for tap in range(9):
        taps[tap] = kernel_of(rows, tap)
    pads = (pad0, pad1, pad2)
    count = per * side * side

    pre = jnp.zeros((count, chans), F32)
    for tap in range(9):
        a, b = divmod(tap, 3)
        window = pads[b][:, a : a + side].reshape(count, chans)
        pre = pre + jnp.dot(window, taps[tap], preferred_element_type=F32)
    gate = jax.nn.sigmoid(pre)
    out = (pre * gate).reshape(pairs, side, 2, side, chans)
    slope = (gate * (1.0 + pre * (1.0 - gate))).reshape(pairs, side, 2, side, chans)
    half = chans // 2
    for p in range(pairs):
        grads = []
        for h in range(2):
            act[2 * p + h] = out[p, :, h].astype(BF16)
            grad = (cot[2 * p + h].astype(F32) * slope[p, :, h]).astype(BF16)
            for n in range(2):
                base = GRADS + (2 * h + n) * pairs * side + p * side
                for message in messages:
                    message[base : base + side] = grad[:, :, n * half : (n + 1) * half]
            grads.append(grad.astype(F32))
        for i in range(side):
            dpre[p, i] = jnp.concatenate([grads[0][i], grads[1][i]], axis=0).astype(BF16)

    lane = lax.broadcasted_iota(jnp.int32, (chans, chans), 1)
    chan = 8 * seat(lane >> 6, (lane >> 3) & 7) + (lane & 7)
    sort = (rows_iota((chans, chans)) == chan).astype(F32).astype(BF16)

    def split(value, groups):
        value = jnp.dot(value, sort, preferred_element_type=F32)
        value = value.reshape(groups, 2, value.shape[0] // (2 * groups), chans)
        parts = []
        for m in range(4):
            span = slice((m >> 1) * half, (m >> 1) * half + half)
            first = value[:, 0, :, span].reshape(-1, half)
            second = value[:, 1, :, span].reshape(-1, half)
            low = lax.broadcasted_iota(jnp.int32, first.shape, 1) < half // 2
            if m & 1:
                first = pltpu.roll(first, half // 2, 1)
            else:
                second = pltpu.roll(second, half // 2, 1)
            parts.append(jnp.where(low, first, second).reshape(-1, 8, half))
        swapped = role & 1 == 1
        parts = [jnp.where(swapped, parts[m ^ 1], parts[m]) for m in range(4)]
        swapped = role >> 1 == 1
        return [jnp.where(swapped, parts[m ^ 2], parts[m]).astype(BF16) for m in range(4)]

    for message, part in zip(messages, split(pad1[...].reshape(-1, chans), pairs * (side + 2))):
        message[0:COLUMNS] = part
    for message, part in zip(messages, split(cols[...].reshape(-1, chans), 2 * pairs)):
        message[COLUMNS:GRADS] = part


def weight_kernel(block0, block1, block2, block3, send, win0, win1, win2, grads):
    half = block0.shape[2]
    pairs, side = 3, 8
    where = rows_iota((side, half))

    for couple, blocks in enumerate(((block0, block1), (block2, block3))):

        def gather(p, c, couple=couple, blocks=blocks):
            u = couple * pairs + p
            for r in range(side + 2):
                shifted = ([], [], [])
                row = slice(r % 8, r % 8 + 1)
                for block in blocks:
                    x = block[p * (side + 2) + r].astype(F32)
                    left = block[COLUMNS + 2 * p + r // 8].astype(F32)[row]
                    right = block[COLUMNS + 2 * (p + pairs) + r // 8].astype(F32)[row]
                    shifted[0].append(jnp.where(where == 0, left, pltpu.roll(x, 1, 0)))
                    shifted[1].append(x)
                    shifted[2].append(
                        jnp.where(where == side - 1, right, pltpu.roll(x, side - 1, 0))
                    )
                for win, parts in zip((win0, win1, win2), shifted):
                    win[u, r] = jnp.concatenate(parts, axis=0).astype(BF16)
            for i in range(side):
                for n in range(4):
                    parts = [
                        block[GRADS + (n * pairs + p) * side + i].astype(F32) for block in blocks
                    ]
                    value = jnp.concatenate(parts, axis=0).astype(BF16)
                    grads[u, i, :, n * half : (n + 1) * half] = value
            return c

        lax.fori_loop(0, pairs, gather, 0)
    flat = grads[...].reshape(-1, 4 * half)
    wins = (win0, win1, win2)
    quarter = half // 2
    for tap in range(9):
        a, b = divmod(tap, 3)
        window = wins[b][:, a : a + side].reshape(-1, half)
        part = lax.dot_general(
            window, flat, (((0,), (0,)), ((), ())), preferred_element_type=F32
        )
        part = part[:quarter, : 2 * half] + part[quarter:, 2 * half :]
        send[:, tap] = part.reshape(8, 8, 2 * half)


def backward_kernel(
    me_ref, route, dpre, taps, send, inner, own_sides, own_corners, acc0, acc1, acc2
):
    pairs, side, chans = dpre.shape[0], dpre.shape[1], dpre.shape[3]
    width = send.shape[0]
    entries = 8 * pairs
    me = me_ref[0]
    where = rows_iota((side, chans))
    flat = dpre[...].reshape(2 * pairs * side * side, chans)
    accs = (acc0, acc1, acc2)
    for acc in accs:
        acc[...] = jnp.zeros_like(acc)
    for tap in range(9):
        a, b = divmod(tap, 3)
        back = lax.dot_general(
            flat, taps[tap], (((1,), (1,)), ((), ())), preferred_element_type=F32
        )
        accs[b][:, a : a + side] += back.reshape(pairs, side, 2 * side, chans)

    def clear(d, c):
        send[d, STRIPS] = jnp.zeros((8, chans), BF16)
        return c

    lax.fori_loop(0, width, clear, 0)

    def borders(p, c):
        for h in range(2):
            t = 2 * p + h
            span = slice(h * side, (h + 1) * side)
            left = jnp.zeros((side, chans), F32)
            right = jnp.zeros((side, chans), F32)
            corner = jnp.zeros((side, chans), F32)
            for r in range(side + 2):
                q0, q1, q2 = (acc[p, r, span] for acc in accs)
                up = jnp.where(where == side - 1, 0.0, pltpu.roll(q0, side - 1, 0))
                down = jnp.where(where == 0, 0.0, pltpu.roll(q2, 1, 0))
                mid = up + q1 + down
                first = jnp.broadcast_to(q0[0:1], (side, chans))
                last = jnp.broadcast_to(q2[side - 1 : side], (side, chans))
                if r == 0 or r == side + 1:
                    e = 0 if r == 0 else 1
                    own_sides[t, e] = mid.astype(BF16)
                    corner = jnp.where(where == 2 * e, first, corner)
                    corner = jnp.where(where == 2 * e + 1, last, corner)
                else:
                    inner[t, r - 1] = mid
                    left = jnp.where(where == r - 1, first, left)
                    right = jnp.where(where == r - 1, last, right)
            own_sides[t, 2] = left.astype(BF16)
            own_sides[t, 3] = right.astype(BF16)
            own_corners[t] = corner.astype(BF16)
        return c

    lax.fori_loop(0, pairs, borders, 0)

    def place(k, c):
        entry = route[k]

        @pl.when(owner_of(entry) != me)
        def _():
            send[owner_of(entry), slot_of(entry)] = own_sides[k >> 2, k & 3]

        corner = route[entries + k]
        owner = owner_of(corner)

        @pl.when((owner != me) & (owner < width))
        def _():
            cell = pick_row(own_corners[k >> 2].astype(F32), k & 3)
            old = send[owner, STRIPS].astype(F32)
            new = jnp.where(rows_iota(old.shape) == slot_of(corner), cell, old)
            send[owner, STRIPS] = new.astype(BF16)

        return c

    lax.fori_loop(0, entries, place, 0)


def sum_kernel(recv, rows, squares):
    g = recv[0]
    for n in range(1, recv.shape[0]):
        g = g + recv[n]
    rows[...] = g
    squares[...] = jnp.full(squares.shape, jnp.sum(g * g), F32)


def final_kernel(
    mine_ref, bit_ref, decay_ref, squares, w, g, w0, w1, g0, g1, ema, averaged, ema_out,
    low, high,
):
    chans = w.shape[1]
    half = chans // 2
    mine = mine_ref[0]
    bit = bit_ref[0]
    decay = decay_ref[0]
    flip = jnp.where(bit == 0, 1, 2)
    number = lax.broadcasted_iota(jnp.int32, squares.shape, 0) // (squares.shape[0] // 4)

    def rms(replica):
        total = jnp.sum(jnp.where(number == replica, squares[...], 0.0), axis=0)
        return jnp.sqrt(total / (9.0 * chans * chans) + 1e-06)

    def ordered(value):
        for n, part in enumerate((low, high)):
            for tap in range(9):
                part[pl.ds(tap, 8, stride=9), :] = value[tap][:, n * half : (n + 1) * half]
        return low[...], high[...]

    own_rms, other_rms = rms(mine), rms(mine ^ flip)
    first = bit == 0
    own = [x for x in ordered(g[...])]
    other = [x for x in ordered(jnp.where(first, g0[...], g1[...]))]
    for n in range(2):
        span = slice(n * half, (n + 1) * half)
        updated = w[:, span] - LEARN * own[n] / own_rms
        partner = jnp.where(first, w0[:, span], w1[:, span]) - LEARN * other[n] / other_rms
        mean = 0.5 * (updated + partner)
        averaged[:, span] = mean
        ema_out[:, span] = decay * ema[:, span] + (1.0 - decay) * mean


def grad_kernel(me_ref, route, inner, own_sides, own_corners, recv, out):
    per, side, chans = inner.shape[0], inner.shape[1], inner.shape[3]
    width = recv.shape[0]
    entries = 4 * per
    me = me_ref[0]
    where = rows_iota((side, chans))

    def tile(t, c):
        sides = []
        for e in range(4):
            entry = route[t * 4 + e]
            owner = owner_of(entry)
            mine = owner == me
            here = own_sides[jnp.where(mine, link_of(entry) - me * per, 0), code_of(entry)]
            there = recv[jnp.where(mine, 0, owner), jnp.where(mine, 0, slot_of(entry))]
            sides.append(jnp.where(mine, here.astype(F32), there.astype(F32)))
        cells = []
        for q in range(4):
            entry = route[entries + t * 4 + q]
            owner = owner_of(entry)
            mine = owner == me
            lost = owner >= width
            here = own_corners[jnp.where(mine, link_of(entry) - me * per, 0)]
            there = recv[jnp.where(mine | lost, 0, owner), STRIPS]
            group = jnp.where(mine, here.astype(F32), there.astype(F32))
            row = jnp.where(lost, -1, jnp.where(mine, code_of(entry), slot_of(entry)))
            cells.append(pick_row(group, row))
        for i in range(side):
            x = inner[t, i]
            if i == 0:
                x = x + sides[0]
            if i == side - 1:
                x = x + sides[1]
            first, last = sides[2][i : i + 1], sides[3][i : i + 1]
            x = x + jnp.where(where == 0, first, jnp.where(where == side - 1, last, 0.0))
            if i == 0 or i == side - 1:
                q = 0 if i == 0 else 2
                x = x + jnp.where(
                    where == 0, cells[q], jnp.where(where == side - 1, cells[q + 1], 0.0)
                )
            out[t, i] = x.astype(BF16)
        return c

    lax.fori_loop(0, per, tile, 0)


def body(
    fields, cotangent, weights, ema, tile_links, tile_codes, corner_links, corner_codes,
    gossip_bit, batch_size,
):
    field, cot, w = fields[0], cotangent[0], weights[0]
    per, side, chans = field.shape[0], field.shape[1], field.shape[3]
    width = lax.axis_size("tile")
    reps = lax.axis_size("rep")
    entries = 4 * per
    me = lax.axis_index("tile").astype(jnp.int32).reshape(1)
    smem = pl.BlockSpec(memory_space=SMEM)
    vmem = pl.BlockSpec(memory_space=pltpu.VMEM)
    sds = jax.ShapeDtypeStruct

    def swap(value, bit):
        return lax.ppermute(value, "rep", [(i, i ^ (1 << bit)) for i in range(reps)])

    def exchange(value, groups=None, axis="tile"):
        return lax.all_to_all(value, axis, 0, 0, axis_index_groups=groups, tiled=True)

    def share(values):
        got = []
        for value, step in zip(values, (1, 8, 9)):
            got.append(lax.ppermute(value, "tile", [(i, i ^ step) for i in range(width)]))
        return got

    w0, w1 = swap(w, 0), swap(w, 1)

    rows = pl.pallas_call(
        taps_kernel,
        name="taps",
        out_shape=sds((8, 9, 8, chans), BF16),
        in_specs=[vmem],
        out_specs=vmem,
        scratch_shapes=[pltpu.VMEM((72, chans // 2), F32)] * 2,
    )(w)
    rows = exchange(rows, PEERS)

    halo_send, strips, route = pl.pallas_call(
        edge_kernel,
        name="edge",
        out_shape=(
            sds((width, HALO, 8, chans), BF16),
            sds((per, 4, side, chans), BF16),
            sds((2 * entries,), jnp.int32),
        ),
        in_specs=[smem] * 5 + [vmem],
        out_specs=(vmem, vmem, smem),
        scratch_shapes=[SMEM((width + 1,), jnp.int32)],
        cost_estimate=pl.CostEstimate(flops=1_000_000, bytes_accessed=8_000_000, transcendentals=0),
    )(me, tile_links.T, tile_codes.T, corner_links.T, corner_codes.T, field)
    halo = exchange(halo_send)
    rows = [rows] + share([rows] * 3)

    pairs = per // 2
    pad = pltpu.VMEM((pairs, side + 2, 2 * side, chans), BF16)
    acc = pltpu.VMEM((pairs, side + 2, 2 * side, chans), F32)
    any_space = pl.BlockSpec(memory_space=pl.ANY)
    message = sds((MESSAGE, 8, chans // 2), BF16)
    act, dpre, taps, *messages = pl.pallas_call(
        forward_kernel,
        name="forward",
        out_shape=(
            sds((per, side, side, chans), BF16),
            sds((pairs, side, 2 * side, chans), BF16),
            sds((9, chans, chans), BF16),
            message, message, message, message,
        ),
        in_specs=[smem] * 2 + [vmem] * 4 + [any_space] * 4,
        out_specs=(vmem,) * 7,
        scratch_shapes=[
            pad, pad, pad,
            pltpu.VMEM((2, pairs, 2, 2 * side, chans), BF16),
            pltpu.VMEM((4, 8, 9, 8, chans), BF16),
            pltpu.SemaphoreType.DMA((4,)),
        ],
    )(me, route, field, strips, cot, halo, *rows)

    blocks = [messages[0]] + share(messages[1:])

    halo_send, inner, own_sides, own_corners = pl.pallas_call(
        backward_kernel,
        name="backward",
        out_shape=(
            sds((width, HALO, 8, chans), BF16),
            sds((per, side, side, chans), F32),
            sds((per, 4, side, chans), BF16),
            sds((per, 8, chans), BF16),
        ),
        in_specs=[smem] * 2 + [vmem] * 2,
        out_specs=(vmem,) * 4,
        scratch_shapes=[acc, acc, acc],
        cost_estimate=pl.CostEstimate(flops=500_000_000, bytes_accessed=8_000_000, transcendentals=0),
    )(me, route, dpre, taps)
    halo = exchange(halo_send)

    win = pltpu.VMEM((6, side + 2, 2 * side, chans // 2), BF16)
    parts = pl.pallas_call(
        weight_kernel,
        name="weight",
        out_shape=sds((8, 9, 8, chans), F32),
        in_specs=[vmem] * 4,
        out_specs=vmem,
        scratch_shapes=[
            win, win, win,
            pltpu.VMEM((6, side, 2 * side, 2 * chans), BF16),
        ],
    )(*blocks)
    parts = exchange(parts, PEERS)

    g, squares = pl.pallas_call(
        sum_kernel,
        name="sum",
        out_shape=(sds((9, 8, chans), F32), sds((4 * width, 1, 128), F32)),
        in_specs=[vmem],
        out_specs=(vmem, vmem),
    )(parts)
    g0, g1 = swap(g, 0), swap(g, 1)
    groups = [[r * width + i for i in range(4 * width)] for r in range(0, reps, 4)]
    squares = exchange(squares, groups, ("rep", "tile"))

    field_grad = pl.pallas_call(
        grad_kernel,
        name="grad",
        out_shape=sds((per, side, side, chans), BF16),
        in_specs=[smem] * 2 + [vmem] * 4,
        out_specs=vmem,
        cost_estimate=pl.CostEstimate(flops=2_000_000, bytes_accessed=4_000_000, transcendentals=0),
    )(me, route, inner, own_sides, own_corners, halo)

    decay = jnp.power(0.99, batch_size.astype(F32) / 32.0)
    mine = (lax.axis_index("rep").astype(jnp.int32) & 3).reshape(1)
    averaged, ema_out = pl.pallas_call(
        final_kernel,
        name="final",
        out_shape=(sds(w.shape, F32), sds(w.shape, F32)),
        in_specs=[smem] * 3 + [vmem] * 8,
        out_specs=(vmem, vmem),
        scratch_shapes=[pltpu.VMEM((72, chans // 2), F32)] * 2,
    )(mine, gossip_bit, decay, squares, w, g, w0, w1, g0, g1, ema[0])
    return act[None], field_grad[None], averaged[None], ema_out[None]


def solution(mesh):
    tiles = P("rep", "tile", None, None, None)
    rows = P("rep", "tile", None)
    return jax.shard_map(
        body,
        mesh=mesh,
        in_specs=(tiles, tiles, rows, rows) + (P(),) * 6,
        out_specs=(tiles, tiles, rows, rows),
        check_vma=False,
    )
```

```python
import jax
import jax.numpy as jnp
from jax import lax
from jax.experimental import pallas as pl
from jax.experimental.pallas import tpu as pltpu
from jax.sharding import PartitionSpec as P


LEARN = 0.5
STRIPS = 5
HALO = STRIPS + 1
F32 = jnp.float32
BF16 = jnp.bfloat16
SMEM = pltpu.SMEM


def rows_iota(shape):
    return lax.broadcasted_iota(jnp.int32, shape, len(shape) - 2)


def pick_row(group, row):
    return jnp.sum(jnp.where(rows_iota(group.shape) == row, group, 0.0), axis=0, keepdims=True)


def count_bits(v):
    v = v - ((v >> 1) & 0x55555555)
    v = (v & 0x33333333) + ((v >> 2) & 0x33333333)
    v = (v + (v >> 4)) & 0x0F0F0F0F
    return (v * 0x01010101) >> 24


def link_of(entry):
    return entry & 255


def code_of(entry):
    return (entry >> 8) & 3


def slot_of(entry):
    return (entry >> 10) & 31


def owner_of(entry):
    return entry >> 16


def build_routes(me, links, codes, route, masks, base, per, width):
    def clear(d, c):
        masks[d] = 0
        return c

    lax.fori_loop(0, width + 1, clear, 0)

    def owner_and_bit(k):
        tile = me * per + (k >> 2)
        link = links[k & 3, tile]
        code = codes[k & 3, tile]
        owner = jnp.where(link < 0, width, (link * 10923) >> 16)
        bit = jnp.where(me < owner, k, (link - owner * per) * 4 + code)
        bit = jnp.where(link < 0, 0, bit)
        return link, code, owner, bit

    def mark(k, c):
        _, _, owner, bit = owner_and_bit(k)
        masks[owner] = masks[owner] | (1 << bit)
        return c

    lax.fori_loop(0, 4 * per, mark, 0)

    def number(k, c):
        link, code, owner, bit = owner_and_bit(k)
        slot = count_bits(masks[owner] & ((1 << bit) - 1))
        route[base + k] = (link & 255) | (code << 8) | (slot << 10) | (owner << 16)
        return c

    lax.fori_loop(0, 4 * per, number, 0)


def taps_kernel(rows, send, low, high):
    scale = (9.0 * rows.shape[1]) ** (-0.5)
    half = rows.shape[1] // 2
    for n, part in enumerate((low, high)):
        part[...] = rows[:, n * half : (n + 1) * half]
    for tap in range(9):
        picked = [part[pl.ds(tap, 8, stride=9), :] for part in (low, high)]
        value = (jnp.concatenate(picked, axis=1) * scale).astype(BF16)
        for n in range(send.shape[0]):
            send[n, tap] = value


def edge_kernel(me_ref, tl, tc, cl, cc, field, send, strips, route, masks):
    per, side = field.shape[0], field.shape[1]
    width = send.shape[0]
    entries = 4 * per
    me = me_ref[0]
    build_routes(me, tl, tc, route, masks, 0, per, width)
    build_routes(me, cl, cc, route, masks, entries, per, width)
    zero = jnp.zeros(send.shape[2:], BF16)

    def clear(d, c):
        send[d, STRIPS] = zero
        return c

    lax.fori_loop(0, width, clear, 0)

    def edges(t, c):
        strips[t, 0] = field[t, 0]
        strips[t, 1] = field[t, side - 1]
        shape = (side, field.shape[3])
        where = rows_iota(shape)
        left = jnp.zeros(shape, F32)
        right = jnp.zeros(shape, F32)
        for i in range(side):
            x = field[t, i].astype(F32)
            left = jnp.where(where == i, jnp.broadcast_to(x[0:1], shape), left)
            right = jnp.where(where == i, jnp.broadcast_to(x[side - 1 : side], shape), right)
        strips[t, 2] = left.astype(BF16)
        strips[t, 3] = right.astype(BF16)
        return c

    lax.fori_loop(0, per, edges, 0)

    def place(k, c):
        entry = route[k]

        @pl.when(owner_of(entry) != me)
        def _():
            send[owner_of(entry), slot_of(entry)] = strips[k >> 2, k & 3]

        corner = route[entries + k]
        owner = owner_of(corner)

        @pl.when((owner != me) & (owner < width))
        def _():
            q = k & 3
            cell = pick_row(strips[k >> 2, q >> 1].astype(F32), (q & 1) * (side - 1))
            old = send[owner, STRIPS].astype(F32)
            new = jnp.where(rows_iota(old.shape) == slot_of(corner), cell, old)
            send[owner, STRIPS] = new.astype(BF16)

        return c

    lax.fori_loop(0, entries, place, 0)


def seat(role, number):
    y = 2 * (number >> 2) + (role >> 1)
    z = 4 * ((number >> 1) & 1) + 2 * (number & 1) + (role & 1)
    return 8 * y + z


PEERS = [[seat(m, n) for n in range(8)] for m in range(4)]
COLUMNS = 30
GRADS = 42
MESSAGE = 138


def place_of(device):
    y, z = divmod(device, 8)
    return 2 * (y & 1) + (z & 1), 4 * (y >> 1) + 2 * (z >> 2) + ((z >> 1) & 1)


def kernel_of(rows, tap):
    parts = []
    for device in range(32):
        role, number = place_of(device)
        parts.append(rows[role, number, tap].astype(F32))
    return jnp.concatenate(parts, axis=0).astype(BF16)


def role_of(me):
    return 2 * ((me >> 3) & 1) + (me & 1)


def forward_kernel(
    me_ref, route, field, strips, cot, recv, rows0, rows1, rows2, rows3,
    act, dpre, taps, message0, message1, message2, message3,
    pad0, pad1, pad2, cols, rows, sems,
):
    per, side = field.shape[0], field.shape[1]
    width, chans = recv.shape[0], field.shape[3]
    entries = 4 * per
    pairs = per // 2
    me = me_ref[0]
    role = role_of(me)
    messages = (message0, message1, message2, message3)
    copies = [
        pltpu.make_async_copy(source, rows.at[role ^ k], sems.at[k])
        for k, source in enumerate((rows0, rows1, rows2, rows3))
    ]
    for copy in copies:
        copy.start()
    where = rows_iota((side, chans))

    def near(owner, link, code, slot):
        mine = owner == me
        here = strips[jnp.where(mine, link - me * per, 0), code]
        there = recv[jnp.where(mine, 0, owner), jnp.where(mine, 0, slot)]
        return jnp.where(mine, here.astype(F32), there.astype(F32))

    def halo(p, c):
        sides, cells = [], []
        for h in range(2):
            t = 2 * p + h
            found = []
            for e in range(4):
                entry = route[t * 4 + e]
                found.append(
                    near(owner_of(entry), link_of(entry), code_of(entry), slot_of(entry))
                )
            corner_rows = []
            for q in range(4):
                entry = route[entries + t * 4 + q]
                owner = owner_of(entry)
                mine = owner == me
                lost = owner >= width
                code = code_of(entry)
                here = strips[jnp.where(mine, link_of(entry) - me * per, 0), code >> 1]
                there = recv[jnp.where(mine | lost, 0, owner), STRIPS]
                group = jnp.where(mine, here.astype(F32), there.astype(F32))
                row = jnp.where(mine, (code & 1) * (side - 1), slot_of(entry))
                row = jnp.where(lost, -1, row)
                corner_rows.append(pick_row(group, row))
            sides.append(found)
            cells.append(corner_rows)
        for h in range(2):
            for n in range(2):
                column, above, below = sides[h][2 + n], cells[h][n], cells[h][2 + n]
                upper = jnp.where(where == 0, above, pltpu.roll(column, 1, 0))
                lower = jnp.where(where == 0, column[side - 1 : side], 0.0)
                lower = jnp.where(where == 1, below, lower)
                cols[n, p, h] = jnp.concatenate([upper, lower], axis=0).astype(BF16)
        for r in range(side + 2):
            shifted = ([], [], [])
            for h in range(2):
                if r == 0:
                    x, before, after = sides[h][0], cells[h][0], cells[h][1]
                elif r == side + 1:
                    x, before, after = sides[h][1], cells[h][2], cells[h][3]
                else:
                    x = field[2 * p + h, r - 1].astype(F32)
                    before, after = sides[h][2][r - 1 : r], sides[h][3][r - 1 : r]
                shifted[0].append(jnp.where(where == 0, before, pltpu.roll(x, 1, 0)))
                shifted[1].append(x)
                shifted[2].append(jnp.where(where == side - 1, after, pltpu.roll(x, side - 1, 0)))
            for pad, halves in zip((pad0, pad1, pad2), shifted):
                pad[p, r] = jnp.concatenate(halves, axis=0).astype(BF16)
        return c

    lax.fori_loop(0, pairs, halo, 0)

    for copy in copies:
        copy.wait()
    for tap in range(9):
        taps[tap] = kernel_of(rows, tap)
    pads = (pad0, pad1, pad2)
    count = per * side * side

    pre = jnp.zeros((count, chans), F32)
    for tap in range(9):
        a, b = divmod(tap, 3)
        window = pads[b][:, a : a + side].reshape(count, chans)
        pre = pre + jnp.dot(window, taps[tap], preferred_element_type=F32)
    gate = jax.nn.sigmoid(pre)
    out = (pre * gate).reshape(pairs, side, 2, side, chans)
    slope = (gate * (1.0 + pre * (1.0 - gate))).reshape(pairs, side, 2, side, chans)
    half = chans // 2
    for p in range(pairs):
        grads = []
        for h in range(2):
            act[2 * p + h] = out[p, :, h].astype(BF16)
            grad = (cot[2 * p + h].astype(F32) * slope[p, :, h]).astype(BF16)
            for n in range(2):
                base = GRADS + (2 * h + n) * pairs * side + p * side
                for message in messages:
                    message[base : base + side] = grad[:, :, n * half : (n + 1) * half]
            grads.append(grad.astype(F32))
        for i in range(side):
            dpre[p, i] = jnp.concatenate([grads[0][i], grads[1][i]], axis=0).astype(BF16)

    lane = lax.broadcasted_iota(jnp.int32, (chans, chans), 1)
    chan = 8 * seat(lane >> 6, (lane >> 3) & 7) + (lane & 7)
    sort = (rows_iota((chans, chans)) == chan).astype(F32).astype(BF16)

    def split(value, groups):
        value = jnp.dot(value, sort, preferred_element_type=F32)
        value = value.reshape(groups, 2, value.shape[0] // (2 * groups), chans)
        parts = []
        for m in range(4):
            span = slice((m >> 1) * half, (m >> 1) * half + half)
            first = value[:, 0, :, span].reshape(-1, half)
            second = value[:, 1, :, span].reshape(-1, half)
            low = lax.broadcasted_iota(jnp.int32, first.shape, 1) < half // 2
            if m & 1:
                first = pltpu.roll(first, half // 2, 1)
            else:
                second = pltpu.roll(second, half // 2, 1)
            parts.append(jnp.where(low, first, second).reshape(-1, 8, half))
        swapped = role & 1 == 1
        parts = [jnp.where(swapped, parts[m ^ 1], parts[m]) for m in range(4)]
        swapped = role >> 1 == 1
        return [jnp.where(swapped, parts[m ^ 2], parts[m]).astype(BF16) for m in range(4)]

    for message, part in zip(messages, split(pad1[...].reshape(-1, chans), pairs * (side + 2))):
        message[0:COLUMNS] = part
    for message, part in zip(messages, split(cols[...].reshape(-1, chans), 2 * pairs)):
        message[COLUMNS:GRADS] = part


def weight_kernel(me_ref, block0, block1, block2, block3, *refs):
    sends, (win0, win1, win2, grads, parts) = refs[:4], refs[4:]
    half = block0.shape[2]
    pairs, side = 3, 8
    where = rows_iota((side, half))

    for couple, blocks in enumerate(((block0, block1), (block2, block3))):

        def gather(p, c, couple=couple, blocks=blocks):
            u = couple * pairs + p
            for r in range(side + 2):
                shifted = ([], [], [])
                row = slice(r % 8, r % 8 + 1)
                for block in blocks:
                    x = block[p * (side + 2) + r].astype(F32)
                    left = block[COLUMNS + 2 * p + r // 8].astype(F32)[row]
                    right = block[COLUMNS + 2 * (p + pairs) + r // 8].astype(F32)[row]
                    shifted[0].append(jnp.where(where == 0, left, pltpu.roll(x, 1, 0)))
                    shifted[1].append(x)
                    shifted[2].append(
                        jnp.where(where == side - 1, right, pltpu.roll(x, side - 1, 0))
                    )
                for win, parts in zip((win0, win1, win2), shifted):
                    win[u, r] = jnp.concatenate(parts, axis=0).astype(BF16)
            for i in range(side):
                for n in range(4):
                    parts = [
                        block[GRADS + (n * pairs + p) * side + i].astype(F32) for block in blocks
                    ]
                    value = jnp.concatenate(parts, axis=0).astype(BF16)
                    grads[u, i, :, n * half : (n + 1) * half] = value
            return c

        lax.fori_loop(0, pairs, gather, 0)
    flat = grads[...].reshape(-1, 4 * half)
    wins = (win0, win1, win2)
    quarter = half // 2
    for tap in range(9):
        a, b = divmod(tap, 3)
        window = wins[b][:, a : a + side].reshape(-1, half)
        part = lax.dot_general(
            window, flat, (((0,), (0,)), ((), ())), preferred_element_type=F32
        )
        part = part[:quarter, : 2 * half] + part[quarter:, 2 * half :]
        parts[:, tap] = part.reshape(8, 8, 2 * half)
    me = me_ref[0]
    number = 4 * (me >> 4) + ((me >> 1) & 3)
    for k, send in enumerate(sends):
        for high in range(2):
            send[high] = parts[number ^ (4 * high + k)]


def backward_kernel(
    me_ref, route, dpre, taps, send, inner, own_sides, own_corners, acc0, acc1, acc2
):
    pairs, side, chans = dpre.shape[0], dpre.shape[1], dpre.shape[3]
    width = send.shape[0]
    entries = 8 * pairs
    me = me_ref[0]
    where = rows_iota((side, chans))
    flat = dpre[...].reshape(2 * pairs * side * side, chans)
    accs = (acc0, acc1, acc2)
    for acc in accs:
        acc[...] = jnp.zeros_like(acc)
    for tap in range(9):
        a, b = divmod(tap, 3)
        back = lax.dot_general(
            flat, taps[tap], (((1,), (1,)), ((), ())), preferred_element_type=F32
        )
        accs[b][:, a : a + side] += back.reshape(pairs, side, 2 * side, chans)

    def clear(d, c):
        send[d, STRIPS] = jnp.zeros((8, chans), BF16)
        return c

    lax.fori_loop(0, width, clear, 0)

    def borders(p, c):
        for h in range(2):
            t = 2 * p + h
            span = slice(h * side, (h + 1) * side)
            left = jnp.zeros((side, chans), F32)
            right = jnp.zeros((side, chans), F32)
            corner = jnp.zeros((side, chans), F32)
            for r in range(side + 2):
                q0, q1, q2 = (acc[p, r, span] for acc in accs)
                up = jnp.where(where == side - 1, 0.0, pltpu.roll(q0, side - 1, 0))
                down = jnp.where(where == 0, 0.0, pltpu.roll(q2, 1, 0))
                mid = up + q1 + down
                first = jnp.broadcast_to(q0[0:1], (side, chans))
                last = jnp.broadcast_to(q2[side - 1 : side], (side, chans))
                if r == 0 or r == side + 1:
                    e = 0 if r == 0 else 1
                    own_sides[t, e] = mid.astype(BF16)
                    corner = jnp.where(where == 2 * e, first, corner)
                    corner = jnp.where(where == 2 * e + 1, last, corner)
                else:
                    inner[t, r - 1] = mid
                    left = jnp.where(where == r - 1, first, left)
                    right = jnp.where(where == r - 1, last, right)
            own_sides[t, 2] = left.astype(BF16)
            own_sides[t, 3] = right.astype(BF16)
            own_corners[t] = corner.astype(BF16)
        return c

    lax.fori_loop(0, pairs, borders, 0)

    def place(k, c):
        entry = route[k]

        @pl.when(owner_of(entry) != me)
        def _():
            send[owner_of(entry), slot_of(entry)] = own_sides[k >> 2, k & 3]

        corner = route[entries + k]
        owner = owner_of(corner)

        @pl.when((owner != me) & (owner < width))
        def _():
            cell = pick_row(own_corners[k >> 2].astype(F32), k & 3)
            old = send[owner, STRIPS].astype(F32)
            new = jnp.where(rows_iota(old.shape) == slot_of(corner), cell, old)
            send[owner, STRIPS] = new.astype(BF16)

        return c

    lax.fori_loop(0, entries, place, 0)


def add_kernel(part0, part1, part2, part3, keep, send):
    for high, out in enumerate((keep, send)):
        out[...] = (part0[high] + part1[high]) + (part2[high] + part3[high])


def sum_kernel(part0, part1, rows, squares):
    g = part0[...] + part1[...]
    rows[...] = g
    squares[...] = jnp.full(squares.shape, jnp.sum(g * g), F32)


def final_kernel(
    mine_ref, bit_ref, decay_ref, squares, w, g, w0, w1, g_other, ema, averaged, ema_out,
    low, high,
):
    chans = w.shape[1]
    half = chans // 2
    mine = mine_ref[0]
    decay = decay_ref[0]
    first = bit_ref[0] == 0
    number = lax.broadcasted_iota(jnp.int32, squares.shape, 0) // (squares.shape[0] // 2)

    def rms(replica):
        total = jnp.sum(jnp.where(number == replica, squares[...], 0.0), axis=0)
        return jnp.sqrt(total / (9.0 * chans * chans) + 1e-06)

    def ordered(value):
        for n, part in enumerate((low, high)):
            for tap in range(9):
                part[pl.ds(tap, 8, stride=9), :] = value[tap][:, n * half : (n + 1) * half]
        return low[...], high[...]

    own_rms, other_rms = rms(mine), rms(1 - mine)
    own, other = ordered(g[...]), ordered(g_other[...])
    for n in range(2):
        span = slice(n * half, (n + 1) * half)
        updated = w[:, span] - LEARN * own[n] / own_rms
        partner = jnp.where(first, w0[:, span], w1[:, span]) - LEARN * other[n] / other_rms
        mean = 0.5 * (updated + partner)
        averaged[:, span] = mean
        ema_out[:, span] = decay * ema[:, span] + (1.0 - decay) * mean


def grad_kernel(me_ref, route, inner, own_sides, own_corners, recv, out):
    per, side, chans = inner.shape[0], inner.shape[1], inner.shape[3]
    width = recv.shape[0]
    entries = 4 * per
    me = me_ref[0]
    where = rows_iota((side, chans))

    def tile(t, c):
        sides = []
        for e in range(4):
            entry = route[t * 4 + e]
            owner = owner_of(entry)
            mine = owner == me
            here = own_sides[jnp.where(mine, link_of(entry) - me * per, 0), code_of(entry)]
            there = recv[jnp.where(mine, 0, owner), jnp.where(mine, 0, slot_of(entry))]
            sides.append(jnp.where(mine, here.astype(F32), there.astype(F32)))
        cells = []
        for q in range(4):
            entry = route[entries + t * 4 + q]
            owner = owner_of(entry)
            mine = owner == me
            lost = owner >= width
            here = own_corners[jnp.where(mine, link_of(entry) - me * per, 0)]
            there = recv[jnp.where(mine | lost, 0, owner), STRIPS]
            group = jnp.where(mine, here.astype(F32), there.astype(F32))
            row = jnp.where(lost, -1, jnp.where(mine, code_of(entry), slot_of(entry)))
            cells.append(pick_row(group, row))
        for i in range(side):
            x = inner[t, i]
            if i == 0:
                x = x + sides[0]
            if i == side - 1:
                x = x + sides[1]
            first, last = sides[2][i : i + 1], sides[3][i : i + 1]
            x = x + jnp.where(where == 0, first, jnp.where(where == side - 1, last, 0.0))
            if i == 0 or i == side - 1:
                q = 0 if i == 0 else 2
                x = x + jnp.where(
                    where == 0, cells[q], jnp.where(where == side - 1, cells[q + 1], 0.0)
                )
            out[t, i] = x.astype(BF16)
        return c

    lax.fori_loop(0, per, tile, 0)


def body(
    fields, cotangent, weights, ema, tile_links, tile_codes, corner_links, corner_codes,
    gossip_bit, batch_size,
):
    field, cot, w = fields[0], cotangent[0], weights[0]
    per, side, chans = field.shape[0], field.shape[1], field.shape[3]
    width = lax.axis_size("tile")
    reps = lax.axis_size("rep")
    entries = 4 * per
    me = lax.axis_index("tile").astype(jnp.int32).reshape(1)
    smem = pl.BlockSpec(memory_space=SMEM)
    vmem = pl.BlockSpec(memory_space=pltpu.VMEM)
    sds = jax.ShapeDtypeStruct

    def swap(value, bit):
        return lax.ppermute(value, "rep", [(i, i ^ (1 << bit)) for i in range(reps)])

    def exchange(value, groups=None, axis="tile"):
        return lax.all_to_all(value, axis, 0, 0, axis_index_groups=groups, tiled=True)

    def share(values, steps=(1, 8, 9)):
        got = []
        for value, step in zip(values, steps):
            got.append(lax.ppermute(value, "tile", [(i, i ^ step) for i in range(width)]))
        return got

    w0, w1 = swap(w, 0), swap(w, 1)

    rows = pl.pallas_call(
        taps_kernel,
        name="taps",
        out_shape=sds((8, 9, 8, chans), BF16),
        in_specs=[vmem],
        out_specs=vmem,
        scratch_shapes=[pltpu.VMEM((72, chans // 2), F32)] * 2,
    )(w)
    rows = exchange(rows, PEERS)

    halo_send, strips, route = pl.pallas_call(
        edge_kernel,
        name="edge",
        out_shape=(
            sds((width, HALO, 8, chans), BF16),
            sds((per, 4, side, chans), BF16),
            sds((2 * entries,), jnp.int32),
        ),
        in_specs=[smem] * 5 + [vmem],
        out_specs=(vmem, vmem, smem),
        scratch_shapes=[SMEM((width + 1,), jnp.int32)],
        cost_estimate=pl.CostEstimate(flops=1_000_000, bytes_accessed=8_000_000, transcendentals=0),
    )(me, tile_links.T, tile_codes.T, corner_links.T, corner_codes.T, field)
    halo = exchange(halo_send)
    rows = [rows] + share([rows] * 3)

    pairs = per // 2
    pad = pltpu.VMEM((pairs, side + 2, 2 * side, chans), BF16)
    acc = pltpu.VMEM((pairs, side + 2, 2 * side, chans), F32)
    any_space = pl.BlockSpec(memory_space=pl.ANY)
    message = sds((MESSAGE, 8, chans // 2), BF16)
    act, dpre, taps, *messages = pl.pallas_call(
        forward_kernel,
        name="forward",
        out_shape=(
            sds((per, side, side, chans), BF16),
            sds((pairs, side, 2 * side, chans), BF16),
            sds((9, chans, chans), BF16),
            message, message, message, message,
        ),
        in_specs=[smem] * 2 + [vmem] * 4 + [any_space] * 4,
        out_specs=(vmem,) * 7,
        scratch_shapes=[
            pad, pad, pad,
            pltpu.VMEM((2, pairs, 2, 2 * side, chans), BF16),
            pltpu.VMEM((4, 8, 9, 8, chans), BF16),
            pltpu.SemaphoreType.DMA((4,)),
        ],
    )(me, route, field, strips, cot, halo, *rows)

    blocks = [messages[0]] + share(messages[1:])

    halo_send, inner, own_sides, own_corners = pl.pallas_call(
        backward_kernel,
        name="backward",
        out_shape=(
            sds((width, HALO, 8, chans), BF16),
            sds((per, side, side, chans), F32),
            sds((per, 4, side, chans), BF16),
            sds((per, 8, chans), BF16),
        ),
        in_specs=[smem] * 2 + [vmem] * 2,
        out_specs=(vmem,) * 4,
        scratch_shapes=[acc, acc, acc],
        cost_estimate=pl.CostEstimate(flops=500_000_000, bytes_accessed=8_000_000, transcendentals=0),
    )(me, route, dpre, taps)
    halo = exchange(halo_send)

    win = pltpu.VMEM((6, side + 2, 2 * side, chans // 2), BF16)
    parts = pl.pallas_call(
        weight_kernel,
        name="weight",
        out_shape=[sds((2, 9, 8, chans), F32)] * 4,
        in_specs=[smem] + [vmem] * 4,
        out_specs=[vmem] * 4,
        scratch_shapes=[
            win, win, win,
            pltpu.VMEM((6, side, 2 * side, 2 * chans), BF16),
            pltpu.VMEM((8, 9, 8, chans), F32),
        ],
    )(me, *blocks)
    parts = [parts[0]] + share(parts[1:], (2, 4, 6))
    keep, pass_on = pl.pallas_call(
        add_kernel,
        name="add",
        out_shape=[sds((9, 8, chans), F32)] * 2,
        in_specs=[vmem] * 4,
        out_specs=[vmem] * 2,
    )(*parts)
    parts = [keep] + share([pass_on], (16,))

    g, squares = pl.pallas_call(
        sum_kernel,
        name="sum",
        out_shape=(sds((9, 8, chans), F32), sds((2 * width, 1, 128), F32)),
        in_specs=[vmem] * 2,
        out_specs=(vmem, vmem),
    )(*parts)
    decay = jnp.power(0.99, batch_size.astype(F32) / 32.0)
    rep = lax.axis_index("rep").astype(jnp.int32)

    def finish(level):
        flip = 1 << level
        groups = [
            [r * width + i for r in (first, first ^ flip) for i in range(width)]
            for first in range(reps)
            if not first & flip
        ]

        def run(g, squares, halo):
            g_other = swap(g, level)
            squares = exchange(squares, groups, ("rep", "tile"))
            field_grad = pl.pallas_call(
                grad_kernel,
                name="grad",
                out_shape=sds((per, side, side, chans), BF16),
                in_specs=[smem] * 2 + [vmem] * 4,
                out_specs=vmem,
                cost_estimate=pl.CostEstimate(
                    flops=2_000_000, bytes_accessed=4_000_000, transcendentals=0
                ),
            )(me, route, inner, own_sides, own_corners, halo)
            mine = ((rep >> level) & 1).reshape(1)
            averaged, ema_out = pl.pallas_call(
                final_kernel,
                name="final",
                out_shape=(sds(w.shape, F32), sds(w.shape, F32)),
                in_specs=[smem] * 3 + [vmem] * 7,
                out_specs=(vmem, vmem),
                scratch_shapes=[pltpu.VMEM((72, chans // 2), F32)] * 2,
            )(mine, gossip_bit, decay, squares, w, g, w0, w1, g_other, ema[0])
            return field_grad, averaged, ema_out

        return run

    field_grad, averaged, ema_out = lax.cond(
        gossip_bit[0] == 0, finish(0), finish(1), g, squares, halo
    )
    return act[None], field_grad[None], averaged[None], ema_out[None]


def solution(mesh):
    tiles = P("rep", "tile", None, None, None)
    rows = P("rep", "tile", None)
    return jax.shard_map(
        body,
        mesh=mesh,
        in_specs=(tiles, tiles, rows, rows) + (P(),) * 6,
        out_specs=(tiles, tiles, rows, rows),
        check_vma=False,
    )
```

```python
import jax
import jax.numpy as jnp
from jax import lax
from jax.experimental import pallas as pl
from jax.experimental.pallas import tpu as pltpu
from jax.sharding import PartitionSpec as P


LEARN = 0.5
STRIPS = 5
HALO = STRIPS + 1
F32 = jnp.float32
BF16 = jnp.bfloat16
SMEM = pltpu.SMEM
LIMIT = pltpu.CompilerParams(vmem_limit_bytes=20 * 2**20)


def rows_iota(shape):
    return lax.broadcasted_iota(jnp.int32, shape, len(shape) - 2)


def pick_row(group, row):
    return jnp.sum(jnp.where(rows_iota(group.shape) == row, group, 0.0), axis=0, keepdims=True)


def count_bits(v):
    v = v - ((v >> 1) & 0x55555555)
    v = (v & 0x33333333) + ((v >> 2) & 0x33333333)
    v = (v + (v >> 4)) & 0x0F0F0F0F
    return (v * 0x01010101) >> 24


def link_of(entry):
    return entry & 255


def code_of(entry):
    return (entry >> 8) & 3


def slot_of(entry):
    return (entry >> 10) & 31


def owner_of(entry):
    return entry >> 16


def build_routes(me, links, codes, route, masks, base, per, width):
    def clear(d, c):
        masks[d] = 0
        return c

    lax.fori_loop(0, width + 1, clear, 0)

    def owner_and_bit(k):
        tile = me * per + (k >> 2)
        link = links[k & 3, tile]
        code = codes[k & 3, tile]
        owner = jnp.where(link < 0, width, (link * 10923) >> 16)
        bit = jnp.where(me < owner, k, (link - owner * per) * 4 + code)
        bit = jnp.where(link < 0, 0, bit)
        return link, code, owner, bit

    def mark(k, c):
        _, _, owner, bit = owner_and_bit(k)
        masks[owner] = masks[owner] | (1 << bit)
        return c

    lax.fori_loop(0, 4 * per, mark, 0)

    def number(k, c):
        link, code, owner, bit = owner_and_bit(k)
        slot = count_bits(masks[owner] & ((1 << bit) - 1))
        route[base + k] = (link & 255) | (code << 8) | (slot << 10) | (owner << 16)
        return c

    lax.fori_loop(0, 4 * per, number, 0)


def taps_kernel(rows, send, grouped, low, high):
    scale = (9.0 * rows.shape[1]) ** (-0.5)
    half = rows.shape[1] // 2
    for n, part in enumerate((low, high)):
        part[...] = rows[:, n * half : (n + 1) * half]
    for tap in range(9):
        picked = [part[pl.ds(tap, 8, stride=9), :] for part in (low, high)]
        value = jnp.concatenate(picked, axis=1)
        grouped[tap] = value
        value = (value * scale).astype(BF16)
        for n in range(send.shape[0]):
            send[n, tap] = value


def edge_kernel(me_ref, tl, tc, cl, cc, field, send, strips, route, masks):
    per, side = field.shape[0], field.shape[1]
    width = send.shape[0]
    entries = 4 * per
    me = me_ref[0]
    build_routes(me, tl, tc, route, masks, 0, per, width)
    build_routes(me, cl, cc, route, masks, entries, per, width)
    zero = jnp.zeros(send.shape[2:], BF16)

    def clear(d, c):
        send[d, STRIPS] = zero
        return c

    lax.fori_loop(0, width, clear, 0)

    def edges(t, c):
        strips[t, 0] = field[t, 0]
        strips[t, 1] = field[t, side - 1]
        shape = (side, field.shape[3])
        where = rows_iota(shape)
        left = jnp.zeros(shape, F32)
        right = jnp.zeros(shape, F32)
        for i in range(side):
            x = field[t, i].astype(F32)
            left = jnp.where(where == i, jnp.broadcast_to(x[0:1], shape), left)
            right = jnp.where(where == i, jnp.broadcast_to(x[side - 1 : side], shape), right)
        strips[t, 2] = left.astype(BF16)
        strips[t, 3] = right.astype(BF16)
        return c

    lax.fori_loop(0, per, edges, 0)

    def place(k, c):
        entry = route[k]

        @pl.when(owner_of(entry) != me)
        def _():
            send[owner_of(entry), slot_of(entry)] = strips[k >> 2, k & 3]

        corner = route[entries + k]
        owner = owner_of(corner)

        @pl.when((owner != me) & (owner < width))
        def _():
            q = k & 3
            cell = pick_row(strips[k >> 2, q >> 1].astype(F32), (q & 1) * (side - 1))
            old = send[owner, STRIPS].astype(F32)
            new = jnp.where(rows_iota(old.shape) == slot_of(corner), cell, old)
            send[owner, STRIPS] = new.astype(BF16)

        return c

    lax.fori_loop(0, entries, place, 0)


def seat(role, number):
    y = 2 * (number >> 2) + (role >> 1)
    z = 4 * ((number >> 1) & 1) + 2 * (number & 1) + (role & 1)
    return 8 * y + z


PEERS = [[seat(m, n) for n in range(8)] for m in range(4)]
COLUMNS = 30
GRADS = 42
MESSAGE = 138


def place_of(device):
    y, z = divmod(device, 8)
    return 2 * (y & 1) + (z & 1), 4 * (y >> 1) + 2 * (z >> 2) + ((z >> 1) & 1)


def kernel_of(rows, tap):
    parts = []
    for device in range(32):
        role, number = place_of(device)
        parts.append(rows[role, number, tap].astype(F32))
    return jnp.concatenate(parts, axis=0).astype(BF16)


def role_of(me):
    return 2 * ((me >> 3) & 1) + (me & 1)


def forward_kernel(
    me_ref, route, field, strips, cot, recv, rows0, rows1, rows2, rows3,
    act, dpre, taps, message0, message1, message2, message3,
    pad0, pad1, pad2, cols, rows, sems,
):
    per, side = field.shape[0], field.shape[1]
    width, chans = recv.shape[0], field.shape[3]
    entries = 4 * per
    pairs = per // 2
    me = me_ref[0]
    role = role_of(me)
    messages = (message0, message1, message2, message3)
    copies = [
        pltpu.make_async_copy(source, rows.at[role ^ k], sems.at[k])
        for k, source in enumerate((rows0, rows1, rows2, rows3))
    ]
    for copy in copies:
        copy.start()
    where = rows_iota((side, chans))

    def near(owner, link, code, slot):
        mine = owner == me
        here = strips[jnp.where(mine, link - me * per, 0), code]
        there = recv[jnp.where(mine, 0, owner), jnp.where(mine, 0, slot)]
        return jnp.where(mine, here.astype(F32), there.astype(F32))

    def halo(p, c):
        sides, cells = [], []
        for h in range(2):
            t = 2 * p + h
            found = []
            for e in range(4):
                entry = route[t * 4 + e]
                found.append(
                    near(owner_of(entry), link_of(entry), code_of(entry), slot_of(entry))
                )
            corner_rows = []
            for q in range(4):
                entry = route[entries + t * 4 + q]
                owner = owner_of(entry)
                mine = owner == me
                lost = owner >= width
                code = code_of(entry)
                here = strips[jnp.where(mine, link_of(entry) - me * per, 0), code >> 1]
                there = recv[jnp.where(mine | lost, 0, owner), STRIPS]
                group = jnp.where(mine, here.astype(F32), there.astype(F32))
                row = jnp.where(mine, (code & 1) * (side - 1), slot_of(entry))
                row = jnp.where(lost, -1, row)
                corner_rows.append(pick_row(group, row))
            sides.append(found)
            cells.append(corner_rows)
        for h in range(2):
            for n in range(2):
                column, above, below = sides[h][2 + n], cells[h][n], cells[h][2 + n]
                upper = jnp.where(where == 0, above, pltpu.roll(column, 1, 0))
                lower = jnp.where(where == 0, column[side - 1 : side], 0.0)
                lower = jnp.where(where == 1, below, lower)
                cols[n, p, h] = jnp.concatenate([upper, lower], axis=0).astype(BF16)
        for r in range(side + 2):
            shifted = ([], [], [])
            for h in range(2):
                if r == 0:
                    x, before, after = sides[h][0], cells[h][0], cells[h][1]
                elif r == side + 1:
                    x, before, after = sides[h][1], cells[h][2], cells[h][3]
                else:
                    x = field[2 * p + h, r - 1].astype(F32)
                    before, after = sides[h][2][r - 1 : r], sides[h][3][r - 1 : r]
                shifted[0].append(jnp.where(where == 0, before, pltpu.roll(x, 1, 0)))
                shifted[1].append(x)
                shifted[2].append(jnp.where(where == side - 1, after, pltpu.roll(x, side - 1, 0)))
            for pad, halves in zip((pad0, pad1, pad2), shifted):
                pad[p, r] = jnp.concatenate(halves, axis=0).astype(BF16)
        return c

    lax.fori_loop(0, pairs, halo, 0)

    for copy in copies:
        copy.wait()
    for tap in range(9):
        taps[tap] = kernel_of(rows, tap)
    pads = (pad0, pad1, pad2)
    count = per * side * side

    pre = jnp.zeros((count, chans), F32)
    for tap in range(9):
        a, b = divmod(tap, 3)
        window = pads[b][:, a : a + side].reshape(count, chans)
        pre = pre + jnp.dot(window, taps[tap], preferred_element_type=F32)
    gate = jax.nn.sigmoid(pre)
    out = (pre * gate).reshape(pairs, side, 2, side, chans)
    slope = (gate * (1.0 + pre * (1.0 - gate))).reshape(pairs, side, 2, side, chans)
    half = chans // 2
    for p in range(pairs):
        grads = []
        for h in range(2):
            act[2 * p + h] = out[p, :, h].astype(BF16)
            grad = (cot[2 * p + h].astype(F32) * slope[p, :, h]).astype(BF16)
            for n in range(2):
                base = GRADS + (2 * h + n) * pairs * side + p * side
                for message in messages:
                    message[base : base + side] = grad[:, :, n * half : (n + 1) * half]
            grads.append(grad.astype(F32))
        for i in range(side):
            dpre[p, i] = jnp.concatenate([grads[0][i], grads[1][i]], axis=0).astype(BF16)

    lane = lax.broadcasted_iota(jnp.int32, (chans, chans), 1)
    chan = 8 * seat(lane >> 6, (lane >> 3) & 7) + (lane & 7)
    sort = (rows_iota((chans, chans)) == chan).astype(F32).astype(BF16)

    def split(value, groups):
        value = jnp.dot(value, sort, preferred_element_type=F32)
        value = value.reshape(groups, 2, value.shape[0] // (2 * groups), chans)
        parts = []
        for m in range(4):
            span = slice((m >> 1) * half, (m >> 1) * half + half)
            first = value[:, 0, :, span].reshape(-1, half)
            second = value[:, 1, :, span].reshape(-1, half)
            low = lax.broadcasted_iota(jnp.int32, first.shape, 1) < half // 2
            if m & 1:
                first = pltpu.roll(first, half // 2, 1)
            else:
                second = pltpu.roll(second, half // 2, 1)
            parts.append(jnp.where(low, first, second).reshape(-1, 8, half))
        swapped = role & 1 == 1
        parts = [jnp.where(swapped, parts[m ^ 1], parts[m]) for m in range(4)]
        swapped = role >> 1 == 1
        return [jnp.where(swapped, parts[m ^ 2], parts[m]).astype(BF16) for m in range(4)]

    for message, part in zip(messages, split(pad1[...].reshape(-1, chans), pairs * (side + 2))):
        message[0:COLUMNS] = part
    for message, part in zip(messages, split(cols[...].reshape(-1, chans), 2 * pairs)):
        message[COLUMNS:GRADS] = part


def weight_kernel(me_ref, block0, block1, block2, block3, *refs):
    sends, (win0, win1, win2, grads, parts) = refs[:4], refs[4:]
    half = block0.shape[2]
    pairs, side = 3, 8
    where = rows_iota((side, half))

    for couple, blocks in enumerate(((block0, block1), (block2, block3))):

        def gather(p, c, couple=couple, blocks=blocks):
            u = couple * pairs + p
            for r in range(side + 2):
                shifted = ([], [], [])
                row = slice(r % 8, r % 8 + 1)
                for block in blocks:
                    x = block[p * (side + 2) + r].astype(F32)
                    left = block[COLUMNS + 2 * p + r // 8].astype(F32)[row]
                    right = block[COLUMNS + 2 * (p + pairs) + r // 8].astype(F32)[row]
                    shifted[0].append(jnp.where(where == 0, left, pltpu.roll(x, 1, 0)))
                    shifted[1].append(x)
                    shifted[2].append(
                        jnp.where(where == side - 1, right, pltpu.roll(x, side - 1, 0))
                    )
                for win, parts in zip((win0, win1, win2), shifted):
                    win[u, r] = jnp.concatenate(parts, axis=0).astype(BF16)
            for i in range(side):
                for n in range(4):
                    parts = [
                        block[GRADS + (n * pairs + p) * side + i].astype(F32) for block in blocks
                    ]
                    value = jnp.concatenate(parts, axis=0).astype(BF16)
                    grads[u, i, :, n * half : (n + 1) * half] = value
            return c

        lax.fori_loop(0, pairs, gather, 0)
    flat = grads[...].reshape(-1, 4 * half)
    wins = (win0, win1, win2)
    quarter = half // 2
    for tap in range(9):
        a, b = divmod(tap, 3)
        window = wins[b][:, a : a + side].reshape(-1, half)
        part = lax.dot_general(
            window, flat, (((0,), (0,)), ((), ())), preferred_element_type=F32
        )
        part = part[:quarter, : 2 * half] + part[quarter:, 2 * half :]
        parts[:, tap] = part.reshape(8, 8, 2 * half)
    me = me_ref[0]
    number = 4 * (me >> 4) + ((me >> 1) & 3)
    for k, send in enumerate(sends):
        for high in range(2):
            send[high] = parts[number ^ (4 * high + k)]


def backward_kernel(
    me_ref, route, dpre, taps, send, inner, own_sides, own_corners, acc0, acc1, acc2
):
    pairs, side, chans = dpre.shape[0], dpre.shape[1], dpre.shape[3]
    width = send.shape[0]
    entries = 8 * pairs
    me = me_ref[0]
    where = rows_iota((side, chans))
    flat = dpre[...].reshape(2 * pairs * side * side, chans)
    accs = (acc0, acc1, acc2)
    for acc in accs:
        acc[...] = jnp.zeros_like(acc)
    for tap in range(9):
        a, b = divmod(tap, 3)
        back = lax.dot_general(
            flat, taps[tap], (((1,), (1,)), ((), ())), preferred_element_type=F32
        )
        accs[b][:, a : a + side] += back.reshape(pairs, side, 2 * side, chans)

    def clear(d, c):
        send[d, STRIPS] = jnp.zeros((8, chans), BF16)
        return c

    lax.fori_loop(0, width, clear, 0)

    def borders(p, c):
        for h in range(2):
            t = 2 * p + h
            span = slice(h * side, (h + 1) * side)
            left = jnp.zeros((side, chans), F32)
            right = jnp.zeros((side, chans), F32)
            corner = jnp.zeros((side, chans), F32)
            for r in range(side + 2):
                q0, q1, q2 = (acc[p, r, span] for acc in accs)
                up = jnp.where(where == side - 1, 0.0, pltpu.roll(q0, side - 1, 0))
                down = jnp.where(where == 0, 0.0, pltpu.roll(q2, 1, 0))
                mid = up + q1 + down
                first = jnp.broadcast_to(q0[0:1], (side, chans))
                last = jnp.broadcast_to(q2[side - 1 : side], (side, chans))
                if r == 0 or r == side + 1:
                    e = 0 if r == 0 else 1
                    own_sides[t, e] = mid.astype(BF16)
                    corner = jnp.where(where == 2 * e, first, corner)
                    corner = jnp.where(where == 2 * e + 1, last, corner)
                else:
                    inner[t, r - 1] = mid
                    left = jnp.where(where == r - 1, first, left)
                    right = jnp.where(where == r - 1, last, right)
            own_sides[t, 2] = left.astype(BF16)
            own_sides[t, 3] = right.astype(BF16)
            own_corners[t] = corner.astype(BF16)
        return c

    lax.fori_loop(0, pairs, borders, 0)

    def place(k, c):
        entry = route[k]

        @pl.when(owner_of(entry) != me)
        def _():
            send[owner_of(entry), slot_of(entry)] = own_sides[k >> 2, k & 3]

        corner = route[entries + k]
        owner = owner_of(corner)

        @pl.when((owner != me) & (owner < width))
        def _():
            cell = pick_row(own_corners[k >> 2].astype(F32), k & 3)
            old = send[owner, STRIPS].astype(F32)
            new = jnp.where(rows_iota(old.shape) == slot_of(corner), cell, old)
            send[owner, STRIPS] = new.astype(BF16)

        return c

    lax.fori_loop(0, entries, place, 0)


def add_kernel(part0, part1, part2, part3, keep, send):
    for high, out in enumerate((keep, send)):
        out[...] = (part0[high] + part1[high]) + (part2[high] + part3[high])


def sum_kernel(part0, part1, grouped, both, squares):
    g = part0[...] + part1[...]
    both[0] = g
    both[1] = grouped[...]
    squares[...] = jnp.full(squares.shape, jnp.sum(g * g), F32)


def final_kernel(mine_ref, decay_ref, squares, own, other, ema, averaged, ema_out, low, high):
    chans = ema.shape[1]
    half = chans // 2
    mine = mine_ref[0]
    decay = decay_ref[0]
    number = lax.broadcasted_iota(jnp.int32, squares.shape, 0) // (squares.shape[0] // 2)

    def rms(replica):
        total = jnp.sum(jnp.where(number == replica, squares[...], 0.0), axis=0)
        root = jnp.sqrt(total / (9.0 * chans * chans) + 1e-06)
        return jnp.concatenate([root, root], axis=1)

    own_rms, other_rms = rms(mine), rms(1 - mine)
    for tap in range(9):
        updated = own[1, tap] - LEARN * own[0, tap] / own_rms
        partner = other[1, tap] - LEARN * other[0, tap] / other_rms
        mean = 0.5 * (updated + partner)
        for n, part in enumerate((low, high)):
            part[pl.ds(tap, 8, stride=9), :] = mean[:, n * half : (n + 1) * half]
    for n, part in enumerate((low, high)):
        span = slice(n * half, (n + 1) * half)
        mean = part[...]
        averaged[:, span] = mean
        ema_out[:, span] = decay * ema[:, span] + (1.0 - decay) * mean


def grad_kernel(me_ref, route, inner, own_sides, own_corners, recv, out):
    per, side, chans = inner.shape[0], inner.shape[1], inner.shape[3]
    width = recv.shape[0]
    entries = 4 * per
    me = me_ref[0]
    where = rows_iota((side, chans))

    def tile(t, c):
        sides = []
        for e in range(4):
            entry = route[t * 4 + e]
            owner = owner_of(entry)
            mine = owner == me
            here = own_sides[jnp.where(mine, link_of(entry) - me * per, 0), code_of(entry)]
            there = recv[jnp.where(mine, 0, owner), jnp.where(mine, 0, slot_of(entry))]
            sides.append(jnp.where(mine, here.astype(F32), there.astype(F32)))
        cells = []
        for q in range(4):
            entry = route[entries + t * 4 + q]
            owner = owner_of(entry)
            mine = owner == me
            lost = owner >= width
            here = own_corners[jnp.where(mine, link_of(entry) - me * per, 0)]
            there = recv[jnp.where(mine | lost, 0, owner), STRIPS]
            group = jnp.where(mine, here.astype(F32), there.astype(F32))
            row = jnp.where(lost, -1, jnp.where(mine, code_of(entry), slot_of(entry)))
            cells.append(pick_row(group, row))
        for i in range(side):
            x = inner[t, i]
            if i == 0:
                x = x + sides[0]
            if i == side - 1:
                x = x + sides[1]
            first, last = sides[2][i : i + 1], sides[3][i : i + 1]
            x = x + jnp.where(where == 0, first, jnp.where(where == side - 1, last, 0.0))
            if i == 0 or i == side - 1:
                q = 0 if i == 0 else 2
                x = x + jnp.where(
                    where == 0, cells[q], jnp.where(where == side - 1, cells[q + 1], 0.0)
                )
            out[t, i] = x.astype(BF16)
        return c

    lax.fori_loop(0, per, tile, 0)


def body(
    fields, cotangent, weights, ema, tile_links, tile_codes, corner_links, corner_codes,
    gossip_bit, batch_size,
):
    field, cot, w = fields[0], cotangent[0], weights[0]
    per, side, chans = field.shape[0], field.shape[1], field.shape[3]
    width = lax.axis_size("tile")
    reps = lax.axis_size("rep")
    entries = 4 * per
    me = lax.axis_index("tile").astype(jnp.int32).reshape(1)
    smem = pl.BlockSpec(memory_space=SMEM)
    vmem = pl.BlockSpec(memory_space=pltpu.VMEM)
    sds = jax.ShapeDtypeStruct

    def swap(value, bit):
        return lax.ppermute(value, "rep", [(i, i ^ (1 << bit)) for i in range(reps)])

    def exchange(value, groups=None, axis="tile"):
        return lax.all_to_all(value, axis, 0, 0, axis_index_groups=groups, tiled=True)

    def share(values, steps=(1, 8, 9)):
        got = []
        for value, step in zip(values, steps):
            got.append(lax.ppermute(value, "tile", [(i, i ^ step) for i in range(width)]))
        return got

    rows, grouped = pl.pallas_call(
        taps_kernel,
        compiler_params=LIMIT,
        name="taps",
        out_shape=(sds((8, 9, 8, chans), BF16), sds((9, 8, chans), F32)),
        in_specs=[vmem],
        out_specs=(vmem, vmem),
        scratch_shapes=[pltpu.VMEM((72, chans // 2), F32)] * 2,
    )(w)
    rows = exchange(rows, PEERS)

    halo_send, strips, route = pl.pallas_call(
        edge_kernel,
        compiler_params=LIMIT,
        name="edge",
        out_shape=(
            sds((width, HALO, 8, chans), BF16),
            sds((per, 4, side, chans), BF16),
            sds((2 * entries,), jnp.int32),
        ),
        in_specs=[smem] * 5 + [vmem],
        out_specs=(vmem, vmem, smem),
        scratch_shapes=[SMEM((width + 1,), jnp.int32)],
        cost_estimate=pl.CostEstimate(flops=1_000_000, bytes_accessed=8_000_000, transcendentals=0),
    )(me, tile_links.T, tile_codes.T, corner_links.T, corner_codes.T, field)
    halo = exchange(halo_send)
    rows = [rows] + share([rows] * 3)

    pairs = per // 2
    pad = pltpu.VMEM((pairs, side + 2, 2 * side, chans), BF16)
    acc = pltpu.VMEM((pairs, side + 2, 2 * side, chans), F32)
    any_space = pl.BlockSpec(memory_space=pl.ANY)
    message = sds((MESSAGE, 8, chans // 2), BF16)
    act, dpre, taps, *messages = pl.pallas_call(
        forward_kernel,
        compiler_params=LIMIT,
        name="forward",
        out_shape=(
            sds((per, side, side, chans), BF16),
            sds((pairs, side, 2 * side, chans), BF16),
            sds((9, chans, chans), BF16),
            message, message, message, message,
        ),
        in_specs=[smem] * 2 + [vmem] * 4 + [any_space] * 4,
        out_specs=(vmem,) * 7,
        scratch_shapes=[
            pad, pad, pad,
            pltpu.VMEM((2, pairs, 2, 2 * side, chans), BF16),
            pltpu.VMEM((4, 8, 9, 8, chans), BF16),
            pltpu.SemaphoreType.DMA((4,)),
        ],
    )(me, route, field, strips, cot, halo, *rows)

    blocks = [messages[0]] + share(messages[1:])

    halo_send, inner, own_sides, own_corners = pl.pallas_call(
        backward_kernel,
        compiler_params=LIMIT,
        name="backward",
        out_shape=(
            sds((width, HALO, 8, chans), BF16),
            sds((per, side, side, chans), F32),
            sds((per, 4, side, chans), BF16),
            sds((per, 8, chans), BF16),
        ),
        in_specs=[smem] * 2 + [vmem] * 2,
        out_specs=(vmem,) * 4,
        scratch_shapes=[acc, acc, acc],
        cost_estimate=pl.CostEstimate(flops=500_000_000, bytes_accessed=8_000_000, transcendentals=0),
    )(me, route, dpre, taps)
    halo = exchange(halo_send)

    win = pltpu.VMEM((6, side + 2, 2 * side, chans // 2), BF16)
    parts = pl.pallas_call(
        weight_kernel,
        compiler_params=LIMIT,
        name="weight",
        out_shape=[sds((2, 9, 8, chans), F32)] * 4,
        in_specs=[smem] + [vmem] * 4,
        out_specs=[vmem] * 4,
        scratch_shapes=[
            win, win, win,
            pltpu.VMEM((6, side, 2 * side, 2 * chans), BF16),
            pltpu.VMEM((8, 9, 8, chans), F32),
        ],
    )(me, *blocks)
    parts = [parts[0]] + share(parts[1:], (2, 4, 6))
    keep, pass_on = pl.pallas_call(
        add_kernel,
        compiler_params=LIMIT,
        name="add",
        out_shape=[sds((9, 8, chans), F32)] * 2,
        in_specs=[vmem] * 4,
        out_specs=[vmem] * 2,
    )(*parts)
    parts = [keep] + share([pass_on], (16,))

    both, squares = pl.pallas_call(
        sum_kernel,
        compiler_params=LIMIT,
        name="sum",
        out_shape=(sds((2, 9, 8, chans), F32), sds((2 * width, 1, 128), F32)),
        in_specs=[vmem] * 3,
        out_specs=(vmem, vmem),
    )(*parts, grouped)
    decay = jnp.power(0.99, batch_size.astype(F32) / 32.0)
    rep = lax.axis_index("rep").astype(jnp.int32)

    def finish(level):
        flip = 1 << level
        groups = [
            [r * width + i for r in (first, first ^ flip) for i in range(width)]
            for first in range(reps)
            if not first & flip
        ]

        def run(own, squares, halo):
            other = swap(own, level)
            squares = exchange(squares, groups, ("rep", "tile"))
            field_grad = pl.pallas_call(
                grad_kernel,
                compiler_params=LIMIT,
        name="grad",
                out_shape=sds((per, side, side, chans), BF16),
                in_specs=[smem] * 2 + [vmem] * 4,
                out_specs=vmem,
                cost_estimate=pl.CostEstimate(
                    flops=2_000_000, bytes_accessed=4_000_000, transcendentals=0
                ),
            )(me, route, inner, own_sides, own_corners, halo)
            mine = ((rep >> level) & 1).reshape(1)
            averaged, ema_out = pl.pallas_call(
                final_kernel,
                compiler_params=LIMIT,
        name="final",
                out_shape=(sds(w.shape, F32), sds(w.shape, F32)),
                in_specs=[smem] * 2 + [vmem] * 4,
                out_specs=(vmem, vmem),
                scratch_shapes=[pltpu.VMEM((72, chans // 2), F32)] * 2,
            )(mine, decay, squares, own, other, ema[0])
            return field_grad, averaged, ema_out

        return run

    field_grad, averaged, ema_out = lax.cond(
        gossip_bit[0] == 0, finish(0), finish(1), both, squares, halo
    )
    return act[None], field_grad[None], averaged[None], ema_out[None]


def solution(mesh):
    tiles = P("rep", "tile", None, None, None)
    rows = P("rep", "tile", None)
    return jax.shard_map(
        body,
        mesh=mesh,
        in_specs=(tiles, tiles, rows, rows) + (P(),) * 6,
        out_specs=(tiles, tiles, rows, rows),
        check_vma=False,
    )
```

```python
import jax
import jax.numpy as jnp
from jax import lax
from jax.experimental import pallas as pl
from jax.experimental.pallas import tpu as pltpu
from jax.sharding import PartitionSpec as P


LEARN = 0.5
STRIPS = 5
HALO = STRIPS + 1
F32 = jnp.float32
BF16 = jnp.bfloat16
SMEM = pltpu.SMEM
LIMIT = pltpu.CompilerParams(vmem_limit_bytes=20 * 2**20)


def rows_iota(shape):
    return lax.broadcasted_iota(jnp.int32, shape, len(shape) - 2)


def pick_row(group, row):
    return jnp.sum(jnp.where(rows_iota(group.shape) == row, group, 0.0), axis=0, keepdims=True)


def count_bits(v):
    v = v - ((v >> 1) & 0x55555555)
    v = (v & 0x33333333) + ((v >> 2) & 0x33333333)
    v = (v + (v >> 4)) & 0x0F0F0F0F
    return (v * 0x01010101) >> 24


def link_of(entry):
    return entry & 255


def code_of(entry):
    return (entry >> 8) & 3


def slot_of(entry):
    return (entry >> 10) & 31


def owner_of(entry):
    return entry >> 16


def build_routes(me, links, codes, route, masks, base, per, width):
    def clear(d, c):
        masks[d] = 0
        return c

    lax.fori_loop(0, width + 1, clear, 0)

    def owner_and_bit(k):
        tile = me * per + (k >> 2)
        link = links[k & 3, tile]
        code = codes[k & 3, tile]
        owner = jnp.where(link < 0, width, (link * 10923) >> 16)
        bit = jnp.where(me < owner, k, (link - owner * per) * 4 + code)
        bit = jnp.where(link < 0, 0, bit)
        return link, code, owner, bit

    def mark(k, c):
        _, _, owner, bit = owner_and_bit(k)
        masks[owner] = masks[owner] | (1 << bit)
        return c

    lax.fori_loop(0, 4 * per, mark, 0)

    def number(k, c):
        link, code, owner, bit = owner_and_bit(k)
        slot = count_bits(masks[owner] & ((1 << bit) - 1))
        route[base + k] = (link & 255) | (code << 8) | (slot << 10) | (owner << 16)
        return c

    lax.fori_loop(0, 4 * per, number, 0)


def taps_kernel(rows, send, grouped, low, high):
    scale = (9.0 * rows.shape[1]) ** (-0.5)
    half = rows.shape[1] // 2
    for n, part in enumerate((low, high)):
        part[...] = rows[:, n * half : (n + 1) * half]
    for tap in range(9):
        picked = [part[pl.ds(tap, 8, stride=9), :] for part in (low, high)]
        value = jnp.concatenate(picked, axis=1)
        grouped[tap] = value
        value = (value * scale).astype(BF16)
        for n in range(send.shape[0]):
            send[n, tap] = value


def edge_kernel(me_ref, tl, tc, cl, cc, field, send, strips, route, masks):
    per, side = field.shape[0], field.shape[1]
    width = send.shape[0]
    entries = 4 * per
    me = me_ref[0]
    build_routes(me, tl, tc, route, masks, 0, per, width)
    build_routes(me, cl, cc, route, masks, entries, per, width)
    zero = jnp.zeros(send.shape[2:], BF16)

    def clear(d, c):
        send[d, STRIPS] = zero
        return c

    lax.fori_loop(0, width, clear, 0)

    def edges(t, c):
        strips[t, 0] = field[t, 0]
        strips[t, 1] = field[t, side - 1]
        shape = (side, field.shape[3])
        where = rows_iota(shape)
        left = jnp.zeros(shape, F32)
        right = jnp.zeros(shape, F32)
        for i in range(side):
            x = field[t, i].astype(F32)
            left = jnp.where(where == i, jnp.broadcast_to(x[0:1], shape), left)
            right = jnp.where(where == i, jnp.broadcast_to(x[side - 1 : side], shape), right)
        strips[t, 2] = left.astype(BF16)
        strips[t, 3] = right.astype(BF16)
        return c

    lax.fori_loop(0, per, edges, 0)

    def place(k, c):
        entry = route[k]

        @pl.when(owner_of(entry) != me)
        def _():
            send[owner_of(entry), slot_of(entry)] = strips[k >> 2, k & 3]

        corner = route[entries + k]
        owner = owner_of(corner)

        @pl.when((owner != me) & (owner < width))
        def _():
            q = k & 3
            cell = pick_row(strips[k >> 2, q >> 1].astype(F32), (q & 1) * (side - 1))
            old = send[owner, STRIPS].astype(F32)
            new = jnp.where(rows_iota(old.shape) == slot_of(corner), cell, old)
            send[owner, STRIPS] = new.astype(BF16)

        return c

    lax.fori_loop(0, entries, place, 0)


def seat(role, number):
    y = 2 * (number >> 2) + (role >> 1)
    z = 4 * ((number >> 1) & 1) + 2 * (number & 1) + (role & 1)
    return 8 * y + z


COLOURS = [[seat(m, n) for m in pair for n in range(8)] for pair in ((0, 3), (1, 2))]
COLUMNS = 30
GRADS = 42
MESSAGE = 138


def place_of(device):
    y, z = divmod(device, 8)
    return 2 * (y & 1) + (z & 1), 4 * (y >> 1) + 2 * (z >> 2) + ((z >> 1) & 1)


def kernel_of(rows, tap):
    parts = []
    for device in range(32):
        role, number = place_of(device)
        parts.append(rows[role, number, tap].astype(F32))
    return jnp.concatenate(parts, axis=0).astype(BF16)


def role_of(me):
    return 2 * ((me >> 3) & 1) + (me & 1)


def forward_kernel(
    me_ref, route, field, strips, cot, recv, rows0, rows1, rows2,
    act, dpre, taps, message0, message1, message2, message3,
    pad0, pad1, pad2, cols, rows, sems,
):
    per, side = field.shape[0], field.shape[1]
    width, chans = recv.shape[0], field.shape[3]
    entries = 4 * per
    pairs = per // 2
    me = me_ref[0]
    role = role_of(me)
    messages = (message0, message1, message2, message3)
    upper = role >> 1
    sources = (
        rows0.at[pl.ds(8 * upper, 8)],
        rows1,
        rows2,
        rows0.at[pl.ds(8 * (1 - upper), 8)],
    )
    copies = [
        pltpu.make_async_copy(source, rows.at[role ^ k], sems.at[k])
        for k, source in enumerate(sources)
    ]
    for copy in copies:
        copy.start()
    where = rows_iota((side, chans))

    def near(owner, link, code, slot):
        mine = owner == me
        here = strips[jnp.where(mine, link - me * per, 0), code]
        there = recv[jnp.where(mine, 0, owner), jnp.where(mine, 0, slot)]
        return jnp.where(mine, here.astype(F32), there.astype(F32))

    def halo(p, c):
        sides, cells = [], []
        for h in range(2):
            t = 2 * p + h
            found = []
            for e in range(4):
                entry = route[t * 4 + e]
                found.append(
                    near(owner_of(entry), link_of(entry), code_of(entry), slot_of(entry))
                )
            corner_rows = []
            for q in range(4):
                entry = route[entries + t * 4 + q]
                owner = owner_of(entry)
                mine = owner == me
                lost = owner >= width
                code = code_of(entry)
                here = strips[jnp.where(mine, link_of(entry) - me * per, 0), code >> 1]
                there = recv[jnp.where(mine | lost, 0, owner), STRIPS]
                group = jnp.where(mine, here.astype(F32), there.astype(F32))
                row = jnp.where(mine, (code & 1) * (side - 1), slot_of(entry))
                row = jnp.where(lost, -1, row)
                corner_rows.append(pick_row(group, row))
            sides.append(found)
            cells.append(corner_rows)
        for h in range(2):
            for n in range(2):
                column, above, below = sides[h][2 + n], cells[h][n], cells[h][2 + n]
                upper = jnp.where(where == 0, above, pltpu.roll(column, 1, 0))
                lower = jnp.where(where == 0, column[side - 1 : side], 0.0)
                lower = jnp.where(where == 1, below, lower)
                cols[n, p, h] = jnp.concatenate([upper, lower], axis=0).astype(BF16)
        for r in range(side + 2):
            shifted = ([], [], [])
            for h in range(2):
                if r == 0:
                    x, before, after = sides[h][0], cells[h][0], cells[h][1]
                elif r == side + 1:
                    x, before, after = sides[h][1], cells[h][2], cells[h][3]
                else:
                    x = field[2 * p + h, r - 1].astype(F32)
                    before, after = sides[h][2][r - 1 : r], sides[h][3][r - 1 : r]
                shifted[0].append(jnp.where(where == 0, before, pltpu.roll(x, 1, 0)))
                shifted[1].append(x)
                shifted[2].append(jnp.where(where == side - 1, after, pltpu.roll(x, side - 1, 0)))
            for pad, halves in zip((pad0, pad1, pad2), shifted):
                pad[p, r] = jnp.concatenate(halves, axis=0).astype(BF16)
        return c

    lax.fori_loop(0, pairs, halo, 0)

    for copy in copies:
        copy.wait()
    for tap in range(9):
        taps[tap] = kernel_of(rows, tap)
    pads = (pad0, pad1, pad2)
    count = per * side * side

    pre = jnp.zeros((count, chans), F32)
    for tap in range(9):
        a, b = divmod(tap, 3)
        window = pads[b][:, a : a + side].reshape(count, chans)
        pre = pre + jnp.dot(window, taps[tap], preferred_element_type=F32)
    gate = jax.nn.sigmoid(pre)
    out = (pre * gate).reshape(pairs, side, 2, side, chans)
    slope = (gate * (1.0 + pre * (1.0 - gate))).reshape(pairs, side, 2, side, chans)
    half = chans // 2
    for p in range(pairs):
        grads = []
        for h in range(2):
            act[2 * p + h] = out[p, :, h].astype(BF16)
            grad = (cot[2 * p + h].astype(F32) * slope[p, :, h]).astype(BF16)
            for n in range(2):
                base = GRADS + (2 * h + n) * pairs * side + p * side
                for message in messages:
                    message[base : base + side] = grad[:, :, n * half : (n + 1) * half]
            grads.append(grad.astype(F32))
        for i in range(side):
            dpre[p, i] = jnp.concatenate([grads[0][i], grads[1][i]], axis=0).astype(BF16)

    lane = lax.broadcasted_iota(jnp.int32, (chans, chans), 1)
    chan = 8 * seat(lane >> 6, (lane >> 3) & 7) + (lane & 7)
    sort = (rows_iota((chans, chans)) == chan).astype(F32).astype(BF16)

    def split(value, groups):
        value = jnp.dot(value, sort, preferred_element_type=F32)
        value = value.reshape(groups, 2, value.shape[0] // (2 * groups), chans)
        parts = []
        for m in range(4):
            span = slice((m >> 1) * half, (m >> 1) * half + half)
            first = value[:, 0, :, span].reshape(-1, half)
            second = value[:, 1, :, span].reshape(-1, half)
            low = lax.broadcasted_iota(jnp.int32, first.shape, 1) < half // 2
            if m & 1:
                first = pltpu.roll(first, half // 2, 1)
            else:
                second = pltpu.roll(second, half // 2, 1)
            parts.append(jnp.where(low, first, second).reshape(-1, 8, half))
        swapped = role & 1 == 1
        parts = [jnp.where(swapped, parts[m ^ 1], parts[m]) for m in range(4)]
        swapped = role >> 1 == 1
        return [jnp.where(swapped, parts[m ^ 2], parts[m]).astype(BF16) for m in range(4)]

    for message, part in zip(messages, split(pad1[...].reshape(-1, chans), pairs * (side + 2))):
        message[0:COLUMNS] = part
    for message, part in zip(messages, split(cols[...].reshape(-1, chans), 2 * pairs)):
        message[COLUMNS:GRADS] = part


def weight_kernel(me_ref, block0, block1, block2, block3, *refs):
    sends, (win0, win1, win2, grads, parts) = refs[:4], refs[4:]
    half = block0.shape[2]
    pairs, side = 3, 8
    where = rows_iota((side, half))

    for couple, blocks in enumerate(((block0, block1), (block2, block3))):

        def gather(p, c, couple=couple, blocks=blocks):
            u = couple * pairs + p
            for r in range(side + 2):
                shifted = ([], [], [])
                row = slice(r % 8, r % 8 + 1)
                for block in blocks:
                    x = block[p * (side + 2) + r].astype(F32)
                    left = block[COLUMNS + 2 * p + r // 8].astype(F32)[row]
                    right = block[COLUMNS + 2 * (p + pairs) + r // 8].astype(F32)[row]
                    shifted[0].append(jnp.where(where == 0, left, pltpu.roll(x, 1, 0)))
                    shifted[1].append(x)
                    shifted[2].append(
                        jnp.where(where == side - 1, right, pltpu.roll(x, side - 1, 0))
                    )
                for win, parts in zip((win0, win1, win2), shifted):
                    win[u, r] = jnp.concatenate(parts, axis=0).astype(BF16)
            for i in range(side):
                for n in range(4):
                    parts = [
                        block[GRADS + (n * pairs + p) * side + i].astype(F32) for block in blocks
                    ]
                    value = jnp.concatenate(parts, axis=0).astype(BF16)
                    grads[u, i, :, n * half : (n + 1) * half] = value
            return c

        lax.fori_loop(0, pairs, gather, 0)
    flat = grads[...].reshape(-1, 4 * half)
    wins = (win0, win1, win2)
    quarter = half // 2
    for tap in range(9):
        a, b = divmod(tap, 3)
        window = wins[b][:, a : a + side].reshape(-1, half)
        part = lax.dot_general(
            window, flat, (((0,), (0,)), ((), ())), preferred_element_type=F32
        )
        part = part[:quarter, : 2 * half] + part[quarter:, 2 * half :]
        parts[:, tap] = part.reshape(8, 8, 2 * half)
    me = me_ref[0]
    number = 4 * (me >> 4) + ((me >> 1) & 3)
    for k, send in enumerate(sends):
        for high in range(2):
            send[high] = parts[number ^ (4 * high + k)]


def backward_kernel(
    me_ref, route, dpre, taps, send, inner, own_sides, own_corners, acc0, acc1, acc2
):
    pairs, side, chans = dpre.shape[0], dpre.shape[1], dpre.shape[3]
    width = send.shape[0]
    entries = 8 * pairs
    me = me_ref[0]
    where = rows_iota((side, chans))
    flat = dpre[...].reshape(2 * pairs * side * side, chans)
    accs = (acc0, acc1, acc2)
    for acc in accs:
        acc[...] = jnp.zeros_like(acc)
    for tap in range(9):
        a, b = divmod(tap, 3)
        back = lax.dot_general(
            flat, taps[tap], (((1,), (1,)), ((), ())), preferred_element_type=F32
        )
        accs[b][:, a : a + side] += back.reshape(pairs, side, 2 * side, chans)

    def clear(d, c):
        send[d, STRIPS] = jnp.zeros((8, chans), BF16)
        return c

    lax.fori_loop(0, width, clear, 0)

    def borders(p, c):
        for h in range(2):
            t = 2 * p + h
            span = slice(h * side, (h + 1) * side)
            left = jnp.zeros((side, chans), F32)
            right = jnp.zeros((side, chans), F32)
            corner = jnp.zeros((side, chans), F32)
            for r in range(side + 2):
                q0, q1, q2 = (acc[p, r, span] for acc in accs)
                up = jnp.where(where == side - 1, 0.0, pltpu.roll(q0, side - 1, 0))
                down = jnp.where(where == 0, 0.0, pltpu.roll(q2, 1, 0))
                mid = up + q1 + down
                first = jnp.broadcast_to(q0[0:1], (side, chans))
                last = jnp.broadcast_to(q2[side - 1 : side], (side, chans))
                if r == 0 or r == side + 1:
                    e = 0 if r == 0 else 1
                    own_sides[t, e] = mid.astype(BF16)
                    corner = jnp.where(where == 2 * e, first, corner)
                    corner = jnp.where(where == 2 * e + 1, last, corner)
                else:
                    inner[t, r - 1] = mid
                    left = jnp.where(where == r - 1, first, left)
                    right = jnp.where(where == r - 1, last, right)
            own_sides[t, 2] = left.astype(BF16)
            own_sides[t, 3] = right.astype(BF16)
            own_corners[t] = corner.astype(BF16)
        return c

    lax.fori_loop(0, pairs, borders, 0)

    def place(k, c):
        entry = route[k]

        @pl.when(owner_of(entry) != me)
        def _():
            send[owner_of(entry), slot_of(entry)] = own_sides[k >> 2, k & 3]

        corner = route[entries + k]
        owner = owner_of(corner)

        @pl.when((owner != me) & (owner < width))
        def _():
            cell = pick_row(own_corners[k >> 2].astype(F32), k & 3)
            old = send[owner, STRIPS].astype(F32)
            new = jnp.where(rows_iota(old.shape) == slot_of(corner), cell, old)
            send[owner, STRIPS] = new.astype(BF16)

        return c

    lax.fori_loop(0, entries, place, 0)


def add_kernel(part0, part1, part2, part3, keep, send):
    for high, out in enumerate((keep, send)):
        out[...] = (part0[high] + part1[high]) + (part2[high] + part3[high])


def sum_kernel(part0, part1, grouped, both, squares):
    g = part0[...] + part1[...]
    both[0] = g
    both[1] = grouped[...]
    squares[...] = jnp.full(squares.shape, jnp.sum(g * g), F32)


def final_kernel(mine_ref, decay_ref, squares, own, other, ema, averaged, ema_out, low, high):
    chans = ema.shape[1]
    half = chans // 2
    mine = mine_ref[0]
    decay = decay_ref[0]
    number = lax.broadcasted_iota(jnp.int32, squares.shape, 0) // (squares.shape[0] // 2)

    def rms(replica):
        total = jnp.sum(jnp.where(number == replica, squares[...], 0.0), axis=0)
        root = jnp.sqrt(total / (9.0 * chans * chans) + 1e-06)
        return jnp.concatenate([root, root], axis=1)

    own_rms, other_rms = rms(mine), rms(1 - mine)
    for tap in range(9):
        updated = own[1, tap] - LEARN * own[0, tap] / own_rms
        partner = other[1, tap] - LEARN * other[0, tap] / other_rms
        mean = 0.5 * (updated + partner)
        for n, part in enumerate((low, high)):
            part[pl.ds(tap, 8, stride=9), :] = mean[:, n * half : (n + 1) * half]
    for n, part in enumerate((low, high)):
        span = slice(n * half, (n + 1) * half)
        mean = part[...]
        averaged[:, span] = mean
        ema_out[:, span] = decay * ema[:, span] + (1.0 - decay) * mean


def grad_kernel(me_ref, route, inner, own_sides, own_corners, recv, out):
    per, side, chans = inner.shape[0], inner.shape[1], inner.shape[3]
    width = recv.shape[0]
    entries = 4 * per
    me = me_ref[0]
    where = rows_iota((side, chans))

    def tile(t, c):
        sides = []
        for e in range(4):
            entry = route[t * 4 + e]
            owner = owner_of(entry)
            mine = owner == me
            here = own_sides[jnp.where(mine, link_of(entry) - me * per, 0), code_of(entry)]
            there = recv[jnp.where(mine, 0, owner), jnp.where(mine, 0, slot_of(entry))]
            sides.append(jnp.where(mine, here.astype(F32), there.astype(F32)))
        cells = []
        for q in range(4):
            entry = route[entries + t * 4 + q]
            owner = owner_of(entry)
            mine = owner == me
            lost = owner >= width
            here = own_corners[jnp.where(mine, link_of(entry) - me * per, 0)]
            there = recv[jnp.where(mine | lost, 0, owner), STRIPS]
            group = jnp.where(mine, here.astype(F32), there.astype(F32))
            row = jnp.where(lost, -1, jnp.where(mine, code_of(entry), slot_of(entry)))
            cells.append(pick_row(group, row))
        for i in range(side):
            x = inner[t, i]
            if i == 0:
                x = x + sides[0]
            if i == side - 1:
                x = x + sides[1]
            first, last = sides[2][i : i + 1], sides[3][i : i + 1]
            x = x + jnp.where(where == 0, first, jnp.where(where == side - 1, last, 0.0))
            if i == 0 or i == side - 1:
                q = 0 if i == 0 else 2
                x = x + jnp.where(
                    where == 0, cells[q], jnp.where(where == side - 1, cells[q + 1], 0.0)
                )
            out[t, i] = x.astype(BF16)
        return c

    lax.fori_loop(0, per, tile, 0)


def body(
    fields, cotangent, weights, ema, tile_links, tile_codes, corner_links, corner_codes,
    gossip_bit, batch_size,
):
    field, cot, w = fields[0], cotangent[0], weights[0]
    per, side, chans = field.shape[0], field.shape[1], field.shape[3]
    width = lax.axis_size("tile")
    reps = lax.axis_size("rep")
    entries = 4 * per
    me = lax.axis_index("tile").astype(jnp.int32).reshape(1)
    smem = pl.BlockSpec(memory_space=SMEM)
    vmem = pl.BlockSpec(memory_space=pltpu.VMEM)
    sds = jax.ShapeDtypeStruct

    def swap(value, bit):
        return lax.ppermute(value, "rep", [(i, i ^ (1 << bit)) for i in range(reps)])

    def exchange(value, groups=None, axis="tile"):
        return lax.all_to_all(value, axis, 0, 0, axis_index_groups=groups, tiled=True)

    def share(values, steps=(1, 8, 9)):
        got = []
        for value, step in zip(values, steps):
            got.append(lax.ppermute(value, "tile", [(i, i ^ step) for i in range(width)]))
        return got

    rows, grouped = pl.pallas_call(
        taps_kernel,
        compiler_params=LIMIT,
        name="taps",
        out_shape=(sds((16, 9, 8, chans), BF16), sds((9, 8, chans), F32)),
        in_specs=[vmem],
        out_specs=(vmem, vmem),
        scratch_shapes=[pltpu.VMEM((72, chans // 2), F32)] * 2,
    )(w)
    rows = exchange(rows, COLOURS)

    halo_send, strips, route = pl.pallas_call(
        edge_kernel,
        compiler_params=LIMIT,
        name="edge",
        out_shape=(
            sds((width, HALO, 8, chans), BF16),
            sds((per, 4, side, chans), BF16),
            sds((2 * entries,), jnp.int32),
        ),
        in_specs=[smem] * 5 + [vmem],
        out_specs=(vmem, vmem, smem),
        scratch_shapes=[SMEM((width + 1,), jnp.int32)],
        cost_estimate=pl.CostEstimate(flops=1_000_000, bytes_accessed=8_000_000, transcendentals=0),
    )(me, tile_links.T, tile_codes.T, corner_links.T, corner_codes.T, field)
    halo = exchange(halo_send)
    kept = lax.dynamic_slice_in_dim(rows, 8 * (role_of(me[0]) >> 1), 8, 0)
    rows = [rows] + share([kept] * 2, (1, 8))

    pairs = per // 2
    pad = pltpu.VMEM((pairs, side + 2, 2 * side, chans), BF16)
    acc = pltpu.VMEM((pairs, side + 2, 2 * side, chans), F32)
    any_space = pl.BlockSpec(memory_space=pl.ANY)
    message = sds((MESSAGE, 8, chans // 2), BF16)
    act, dpre, taps, *messages = pl.pallas_call(
        forward_kernel,
        compiler_params=LIMIT,
        name="forward",
        out_shape=(
            sds((per, side, side, chans), BF16),
            sds((pairs, side, 2 * side, chans), BF16),
            sds((9, chans, chans), BF16),
            message, message, message, message,
        ),
        in_specs=[smem] * 2 + [vmem] * 4 + [any_space] * 3,
        out_specs=(vmem,) * 7,
        scratch_shapes=[
            pad, pad, pad,
            pltpu.VMEM((2, pairs, 2, 2 * side, chans), BF16),
            pltpu.VMEM((4, 8, 9, 8, chans), BF16),
            pltpu.SemaphoreType.DMA((4,)),
        ],
    )(me, route, field, strips, cot, halo, *rows)

    blocks = [messages[0]] + share(messages[1:])

    halo_send, inner, own_sides, own_corners = pl.pallas_call(
        backward_kernel,
        compiler_params=LIMIT,
        name="backward",
        out_shape=(
            sds((width, HALO, 8, chans), BF16),
            sds((per, side, side, chans), F32),
            sds((per, 4, side, chans), BF16),
            sds((per, 8, chans), BF16),
        ),
        in_specs=[smem] * 2 + [vmem] * 2,
        out_specs=(vmem,) * 4,
        scratch_shapes=[acc, acc, acc],
        cost_estimate=pl.CostEstimate(flops=500_000_000, bytes_accessed=8_000_000, transcendentals=0),
    )(me, route, dpre, taps)
    halo = exchange(halo_send)

    win = pltpu.VMEM((6, side + 2, 2 * side, chans // 2), BF16)
    parts = pl.pallas_call(
        weight_kernel,
        compiler_params=LIMIT,
        name="weight",
        out_shape=[sds((2, 9, 8, chans), F32)] * 4,
        in_specs=[smem] + [vmem] * 4,
        out_specs=[vmem] * 4,
        scratch_shapes=[
            win, win, win,
            pltpu.VMEM((6, side, 2 * side, 2 * chans), BF16),
            pltpu.VMEM((8, 9, 8, chans), F32),
        ],
    )(me, *blocks)
    parts = [parts[0]] + share(parts[1:], (2, 4, 6))
    keep, pass_on = pl.pallas_call(
        add_kernel,
        compiler_params=LIMIT,
        name="add",
        out_shape=[sds((9, 8, chans), F32)] * 2,
        in_specs=[vmem] * 4,
        out_specs=[vmem] * 2,
    )(*parts)
    parts = [keep] + share([pass_on], (16,))

    both, squares = pl.pallas_call(
        sum_kernel,
        compiler_params=LIMIT,
        name="sum",
        out_shape=(sds((2, 9, 8, chans), F32), sds((2 * width, 1, 128), F32)),
        in_specs=[vmem] * 3,
        out_specs=(vmem, vmem),
    )(*parts, grouped)
    decay = jnp.power(0.99, batch_size.astype(F32) / 32.0)
    rep = lax.axis_index("rep").astype(jnp.int32)

    def finish(level):
        flip = 1 << level
        groups = [
            [r * width + i for r in (first, first ^ flip) for i in range(width)]
            for first in range(reps)
            if not first & flip
        ]

        def run(own, squares, halo):
            other = swap(own, level)
            squares = exchange(squares, groups, ("rep", "tile"))
            field_grad = pl.pallas_call(
                grad_kernel,
                compiler_params=LIMIT,
        name="grad",
                out_shape=sds((per, side, side, chans), BF16),
                in_specs=[smem] * 2 + [vmem] * 4,
                out_specs=vmem,
                cost_estimate=pl.CostEstimate(
                    flops=2_000_000, bytes_accessed=4_000_000, transcendentals=0
                ),
            )(me, route, inner, own_sides, own_corners, halo)
            mine = ((rep >> level) & 1).reshape(1)
            averaged, ema_out = pl.pallas_call(
                final_kernel,
                compiler_params=LIMIT,
        name="final",
                out_shape=(sds(w.shape, F32), sds(w.shape, F32)),
                in_specs=[smem] * 2 + [vmem] * 4,
                out_specs=(vmem, vmem),
                scratch_shapes=[pltpu.VMEM((72, chans // 2), F32)] * 2,
            )(mine, decay, squares, own, other, ema[0])
            return field_grad, averaged, ema_out

        return run

    field_grad, averaged, ema_out = lax.cond(
        gossip_bit[0] == 0, finish(0), finish(1), both, squares, halo
    )
    return act[None], field_grad[None], averaged[None], ema_out[None]


def solution(mesh):
    tiles = P("rep", "tile", None, None, None)
    rows = P("rep", "tile", None)
    return jax.shard_map(
        body,
        mesh=mesh,
        in_specs=(tiles, tiles, rows, rows) + (P(),) * 6,
        out_specs=(tiles, tiles, rows, rows),
        check_vma=False,
    )
```
